32 devices in a mesh: row: 8 (over z, core), col: 4 (over y, x).
Axes of the slice: x: 2, y: 2, z: 4, core: 2. Of those that a mesh axis runs over, the one named last changes fastest.
Arguments:
- gram: float32 [8, 4, 2048, 4096], P('row', 'col'), may hold values from -21834.348 to 21835.348, as said below
Outputs:
- factored: float32 [8, 4, 2048, 4096], P('row', 'col')
The draws below stay inside these ranges and needn't reach their ends.
Inputs may be any that keep to these rules, and one draw needn't show every extreme that they name: gram holds a symmetric positive definite matrix of order 16384 whose smallest eigenvalue is at least 1.
All inputs are finite; a program needn't handle non-finite values.
Results may differ from the reference program's by a relative error of at most 0.0001.
Values sent between devices are 32-bit elements; how exact they have to be, the bound alone decides.
A program may use at most 192 MiB of HBM per device.

```python
import math
import jax
import jax.numpy as jnp
from jax import lax

BS = 256
PANELS = 3
ORDER = 16384
RBLK = 8
CBLK = 16
N_ROW = 8
N_COL = 4


def draw_gram(key, part):
    first_key = jax.random.fold_in(jax.random.fold_in(key, 17), 0)
    inner = ORDER // 4
    window = BS // 2
    noise = jax.random.truncated_normal(first_key, -6.0, 6.0, (ORDER, inner), jnp.float32)
    padded = jnp.concatenate([jnp.zeros((window, inner), jnp.float32), noise], axis=0)
    running = jnp.concatenate([jnp.zeros((1, inner), jnp.float32), jnp.cumsum(padded, axis=0)], axis=0)
    recent = (running[window:window + ORDER] - running[0:ORDER]) / math.sqrt(window)
    factor = noise + recent
    product = jnp.dot(factor, factor.T, precision=lax.Precision.HIGHEST, preferred_element_type=jnp.float32)
    symmetric = product / inner + jnp.eye(ORDER, dtype=jnp.float32)
    return symmetric.reshape(RBLK, N_ROW, BS, CBLK, N_COL, BS).transpose(1, 4, 0, 2, 3, 5).reshape(N_ROW, N_COL, RBLK * BS, CBLK * BS)


def setup_inputs(seed: int = 0) -> dict:
    seeds = jax.random.split(jax.random.key(seed), 2)
    return {
        "gram": draw_gram(jax.random.fold_in(seeds[1], 71), 0),
    }


def reference(gram):
    matrix = gram.reshape(N_ROW, N_COL, RBLK, BS, CBLK, BS).transpose(2, 0, 3, 4, 1, 5).reshape(ORDER, ORDER)
    for panel_step in range(PANELS):
        start = panel_step * BS
        stop = start + BS
        diagonal = jnp.linalg.cholesky(matrix[start:stop, start:stop])
        below = matrix[stop:, start:stop]
        panel = lax.linalg.triangular_solve(diagonal, below, left_side=False, lower=True, transpose_a=True)
        update = jnp.dot(panel.astype(jnp.float32), panel.T.astype(jnp.float32), precision=lax.Precision.HIGHEST, preferred_element_type=jnp.float32)
        matrix = matrix.at[stop:, stop:].set(matrix[stop:, stop:] - update)
        matrix = matrix.at[start:stop, start:stop].set(diagonal)
        matrix = matrix.at[stop:, start:stop].set(panel)
        matrix = matrix.at[start:stop, stop:].set(jnp.zeros((BS, ORDER - stop), jnp.float32))
    return matrix.reshape(RBLK, N_ROW, BS, CBLK, N_COL, BS).transpose(1, 4, 0, 2, 3, 5).reshape(N_ROW, N_COL, RBLK * BS, CBLK * BS)
```

```python
import functools

import jax
import jax.numpy as jnp
from jax import lax
from jax.experimental import pallas as pl
from jax.experimental.pallas import tpu as pltpu
from jax.sharding import PartitionSpec as P

BS = 256
PANELS = 3
WIDTH = BS * PANELS
GROUP = 64
CORES = 2
LAG = 2
HI = lax.Precision.HIGHEST
MESH = pl.DeviceIdType.MESH
PAIRS = [(row, col) for col in range(PANELS) for row in range(col, PANELS)]


def lanes(col):
    return jnp.broadcast_to(col, (8, 128))

def eliminate(x, width):
    lane = lax.broadcasted_iota(jnp.int32, (8, 128), 1)
    sub = lax.broadcasted_iota(jnp.int32, (8, 128), 0)
    n = GROUP // 8
    nl = width // 128
    v = [[x[8*r:8*r+8, 128*l:128*l+128] for l in range(nl)] for r in range(n)]
    for r in range(n):
        base = 8 * r
        cols = {q: [lanes(v[q][0][:, base+j:base+j+1]) for j in range(8)] for q in range(r, n)}
        s = {(i, l): lanes(cols[r][l][i:i+1, :]) for i in range(8) for l in range(i, 8)}
        rows = [[lanes(v[r][l][j:j+1, :]) for l in range(nl)] for j in range(8)]
        inv = []
        unit = {}
        mult = {}
        for j in range(8):
            d = s[j, j]
            inv.append(recip(d))
            for i in range(j + 1, 8):
                f = s[j, i] * inv[j]
                mult[i, j] = f
                for l in range(i, 8):
                    s[i, l] = s[i, l] - f * s[j, l]
        for i in range(8):
            for l in range(i):
                t = mult[i, l]
                for m in range(l + 1, i):
                    t = t + mult[i, m] * unit[m, l]
                unit[i, l] = -t
        wcol = []
        for j in range(8):
            t = jnp.where(sub == j, 1.0, 0.0)
            for i in range(j + 1, 8):
                t = jnp.where(sub == i, unit[i, j], t)
            wcol.append(t)
        dvec = s[0, 0]
        for j in range(1, 8):
            dvec = jnp.where(sub == j, s[j, j], dvec)
        scale = lax.rsqrt(dvec)
        ident = [jnp.where((lane >= base) & (lane < base + 8), jnp.where(lane == base + j, 1.0, 0.0), rows[j][0]) for j in range(8)]
        for q in range(r + 1, n):
            c = list(cols[q])
            f = []
            for j in range(8):
                fj = c[j] * inv[j]
                f.append(fj)
                for l in range(j + 1, 8):
                    c[l] = c[l] - fj * s[j, l]
            first = jnp.where((lane >= base) & (lane < base + 8), 0.0, v[q][0])
            acc = [first] + [v[q][l] for l in range(1, nl)]
            for j in range(8):
                g = f[j]
                for i in range(j + 1, 8):
                    g = g + f[i] * unit[i, j]
                acc[0] = acc[0] - g * ident[j]
                for l in range(1, nl):
                    acc[l] = acc[l] - g * rows[j][l]
            v[q] = acc
        new = []
        for l in range(nl):
            t = wcol[0] * (ident[0] if l == 0 else rows[0][l])
            for j in range(1, 8):
                t = t + wcol[j] * (ident[j] if l == 0 else rows[j][l])
            new.append(t * scale)
        upper = wcol[0] * rows[0][0]
        for j in range(1, 8):
            upper = upper + wcol[j] * rows[j][0]
        keep = (lane > base + sub) & (lane < base + 8)
        new[0] = jnp.where(keep, upper * scale, new[0])
        v[r] = new
    return jnp.concatenate([jnp.concatenate(t, axis=1) for t in v], axis=0)

def recip(d):
    r = pl.reciprocal(d, approx=True)
    r = r * (2.0 - d * r)
    return r

def factor(m, bs, panels, hook=None):
    width = bs * panels
    groups = bs // GROUP
    for k in range(panels):
        def body(g, carry):
            start = pl.multiple_of(k * bs + g * GROUP, GROUP)
            rows = m[pl.ds(start, GROUP), :]
            x = pltpu.roll(rows, width - start, axis=1)
            x = eliminate(x, width)
            x = pltpu.roll(x, start, axis=1)
            m[pl.ds(start, GROUP), :] = x
            lane = lax.broadcasted_iota(jnp.int32, (GROUP, width), 1)
            sub = lax.broadcasted_iota(jnp.int32, (GROUP, width), 0)
            upd = jnp.where((lane - start > sub) & (lane < start + GROUP), 0.0, x)
            own = x[:, k*bs:(k+1)*bs]
            lane_own = lax.broadcasted_iota(jnp.int32, (GROUP, bs), 1) + k * bs
            left = jnp.where(lane_own >= start + GROUP, own, 0.0)
            prod = lax.dot_general(left, upd, (((0,), (0,)), ((), ())), precision=HI, preferred_element_type=jnp.float32)
            old = m[k*bs:(k+1)*bs, :]
            r2 = lax.broadcasted_iota(jnp.int32, (bs, width), 0) + k * bs
            l2 = lax.broadcasted_iota(jnp.int32, (bs, width), 1)
            old = jnp.where((r2 >= start + GROUP) & (l2 >= start) & (l2 < start + GROUP), 0.0, old)
            m[k*bs:(k+1)*bs, :] = old - prod
            if hook is not None: hook(k * groups + g)
            return carry
        lax.fori_loop(0, groups, body, 0)
        if k + 1 < panels:
            full = m[k*bs:(k+1)*bs, :]
            l2 = lax.broadcasted_iota(jnp.int32, (bs, width), 1)
            r2 = lax.broadcasted_iota(jnp.int32, (bs, width), 0) + k * bs
            upd = jnp.where((l2 > r2) & (l2 < (k+1)*bs), 0.0, full)
            for r in range(k + 1, panels):
                left = m[k*bs:(k+1)*bs, r*bs:(r+1)*bs]
                prod = lax.dot_general(left, upd, (((0,), (0,)), ((), ())), precision=HI, preferred_element_type=jnp.float32)
                if k > 0:
                    m[r*bs:(r+1)*bs, :k*bs] -= prod[:, :k*bs]
                m[r*bs:(r+1)*bs, k*bs:(k+1)*bs] = -prod[:, k*bs:(k+1)*bs]
                m[r*bs:(r+1)*bs, (k+1)*bs:] -= prod[:, (k+1)*bs:]

def exchange_kernel(
    grid_rows, grid_cols, blocks, matrix, raw, corner,
    stage, stage_sem, corner_send, corner_recv, left_send, left_recv, right_send, right_recv,
):
    own_row, own_col = lax.axis_index("row"), lax.axis_index("col")
    ratio = grid_rows // grid_cols
    core = lax.rem(own_row, CORES)
    steps = blocks * PANELS
    has_up, has_down = own_row + CORES < grid_rows, own_row >= CORES
    up = jnp.minimum(own_row + CORES, grid_rows - CORES + core)
    down = jnp.maximum(own_row - CORES, core)
    partner = own_row + 1 - 2 * core

    barrier = pltpu.get_barrier_semaphore()
    for other in range(1, grid_cols):
        pl.semaphore_signal(
            barrier, inc=1, device_id=(own_row, lax.rem(own_col + other, grid_cols)), device_id_type=MESH
        )
    pl.semaphore_signal(barrier, inc=1, device_id=(partner, own_col), device_id_type=MESH)

    @pl.when(has_up)
    def _():
        pl.semaphore_signal(barrier, inc=1, device_id=(up, own_col), device_id_type=MESH)

    @pl.when(has_down)
    def _():
        pl.semaphore_signal(barrier, inc=1, device_id=(down, own_col), device_id_type=MESH)

    pl.semaphore_wait(
        barrier, grid_cols + has_up.astype(jnp.int32) + has_down.astype(jnp.int32)
    )

    def copy(src, dst, send, recv, row, col):
        return pltpu.make_async_remote_copy(
            src_ref=src, dst_ref=dst, send_sem=send, recv_sem=recv,
            device_id=(row, col), device_id_type=MESH,
        )

    fetch = pltpu.make_async_copy(matrix.at[:, 0:BS], stage, stage_sem)

    @pl.when(own_col < PANELS)
    def _():
        fetch.start()

    half = BS // 2

    def corner_part(n, part, start, relays):
        row, col = PAIRS[n]
        span = pl.ds(part * half, half)
        slot = 2 * n + part
        here = corner.at[n, span]
        sends = corner_send.at[slot]
        root = (own_row == row) & (own_col == col)
        primary = core == row % CORES
        line = primary & (own_col == col)

        def send(src, index, to_row, to_col):
            c = copy(src, here, sends.at[index], corner_recv.at[slot], to_row, to_col)
            if start:
                c.start()
            else:
                c.wait_send()

        def fan(src, go_up, go_down):
            @pl.when(go_up)
            def _():
                send(src, 0, up, own_col)

            @pl.when(go_down)
            def _():
                send(src, 1, down, own_col)

            for other in range(1, grid_cols):
                send(src, 2 + other, own_row, lax.rem(own_col + other, grid_cols))

        if relays:
            @pl.when(root)
            def _():
                src = matrix.at[span, 0:BS]
                fan(src, has_up, has_down)
                send(src, 2, partner, own_col)

        @pl.when(jnp.logical_not(root) & (line if relays else jnp.logical_not(line)))
        def _():
            if start:
                copy(here, here, sends.at[2], corner_recv.at[slot], partner, own_col).wait_recv()
            if relays:
                fan(here, has_up & (own_row > row), has_down & (own_row < row))

            @pl.when(primary)
            def _():
                send(here, 2, partner, own_col)

    def corner_pass(start, relays):
        for n in range(len(PAIRS)):
            for part in range(2):
                corner_part(n, part, start, relays)

    corner_pass(True, True)
    corner_pass(True, False)

    @pl.when(own_col < PANELS)
    def _():
        fetch.wait()
        for n, (row, col) in enumerate(PAIRS):
            @pl.when((own_row == row) & (own_col == col))
            def _():
                keep = pltpu.make_async_copy(stage.at[0:BS], corner.at[n], stage_sem)
                keep.start()
                keep.wait()
        for k in range(PANELS):
            @pl.when(own_col == k)
            def _():
                pltpu.make_async_copy(stage, raw.at[0, :, k * BS : (k + 1) * BS], stage_sem).start()

    root_col = lax.rem(own_row, grid_cols)

    def tile(slot, i, k):
        return raw.at[slot, pl.ds(pl.multiple_of(i * BS, BS), BS), pl.ds(pl.multiple_of(k * BS, BS), BS)]

    def left(i, other, k):
        col = lax.rem(root_col + other, grid_cols)
        return col, copy(
            stage.at[pl.ds(pl.multiple_of(i * BS, BS), BS)], tile(0, i, k),
            left_send.at[other, i], left_recv.at[i * PANELS + k], own_row, col,
        )

    def each_left(act):
        for other in range(grid_cols):
            def one(i, carry, other=other):
                for k in range(PANELS):
                    @pl.when(own_col == k)
                    def _():
                        col, c = left(i, other, k)

                        @pl.when(col != own_col)
                        def _():
                            act(c)
                return carry
            lax.fori_loop(0, blocks, one, 0)

    each_left(lambda c: c.start())

    active = core == lax.rem(own_col, CORES)

    plane, planes = own_row // CORES, grid_rows // CORES

    def right(turn, start):
        if start:
            @pl.when(turn < steps)
            def _():
                k = lax.rem(turn, PANELS)

                @pl.when(own_col != k)
                def _():
                    here = tile(0, turn // PANELS, k)
                    copy(here, here, left_send.at[0, 0], left_recv.at[turn], partner, own_col).wait_recv()

                @pl.when((own_col == k) & (turn == k))
                def _():
                    pltpu.make_async_copy(stage, raw.at[0, :, 0:BS], stage_sem).wait()
        for t in range(ratio):
            source = own_col + grid_cols * t
            root = own_row == source
            step = turn - LAG * jnp.abs(plane - source // CORES)

            @pl.when((step >= 0) & (step < steps))
            def _():
                i, k = step // PANELS, lax.rem(step, PANELS)
                here = tile(1 + t, i, k)

                def send(src, index, to_row):
                    c = copy(src, here, right_send.at[t, index, step], right_recv.at[t, step], to_row, own_col)
                    if start:
                        c.start()
                    else:
                        c.wait_send()

                def fan(src, go_up, go_down):
                    @pl.when(go_up)
                    def _():
                        send(src, 0, up)

                    @pl.when(go_down)
                    def _():
                        send(src, 1, down)

                    send(src, 2, partner)

                @pl.when(root)
                def _():
                    fan(tile(0, i, k), has_up, has_down)

                @pl.when(jnp.logical_not(root))
                def _():
                    if start:
                        copy(
                            here, here, right_send.at[t, 2, step], right_recv.at[t, step], partner, own_col
                        ).wait_recv()

                    @pl.when(active)
                    def _():
                        fan(here, has_up & (own_row > source), has_down & (own_row < source))

    def go(turn, carry):
        right(turn, True)
        return carry

    def finish(turn, carry):
        right(turn, False)
        return carry

    turns = steps + LAG * (planes - 1)
    lax.fori_loop(0, turns, go, 0)
    lax.fori_loop(0, turns, finish, 0)
    each_left(lambda c: c.wait_send())
    corner_pass(False, True)
    corner_pass(False, False)


def exchange(grid_rows, grid_cols, matrix):
    rows = matrix.shape[0]
    blocks = rows // BS
    ratio = grid_rows // grid_cols
    steps = blocks * PANELS
    dma = pltpu.SemaphoreType.DMA
    return pl.pallas_call(
        functools.partial(exchange_kernel, grid_rows, grid_cols, blocks),
        out_shape=(
            jax.ShapeDtypeStruct((1 + ratio, rows, WIDTH), jnp.float32),
            jax.ShapeDtypeStruct((len(PAIRS), BS, BS), jnp.float32),
        ),
        in_specs=[pl.BlockSpec(memory_space=pltpu.HBM)],
        out_specs=(pl.BlockSpec(memory_space=pltpu.HBM), pl.BlockSpec(memory_space=pltpu.HBM)),
        scratch_shapes=[
            pltpu.VMEM((rows, BS), jnp.float32),
            dma,
            dma((2 * len(PAIRS), 2 + grid_cols)),
            dma((2 * len(PAIRS),)),
            dma((grid_cols, blocks)),
            dma((steps,)),
            dma((ratio, 3, steps)),
            dma((ratio, steps)),
        ],
        compiler_params=pltpu.CompilerParams(collective_id=0, has_side_effects=True),
        name="exchange",
    )(matrix)


def corner_kernel(corner, high, low, m):
    for n, (row, col) in enumerate(PAIRS):
        block = corner[n]
        m[col * BS : (col + 1) * BS, row * BS : (row + 1) * BS] = block.T
        if row != col:
            m[row * BS : (row + 1) * BS, col * BS : (col + 1) * BS] = block
    factor(m, BS, PANELS)
    for k in range(PANELS):
        rows = m[k * BS : (k + 1) * BS, :]
        lane = lax.broadcasted_iota(jnp.int32, rows.shape, 1)
        sub = lax.broadcasted_iota(jnp.int32, rows.shape, 0) + k * BS
        rows = jnp.where(lane > sub, 0.0, rows)
        top = rows.astype(jnp.bfloat16)
        high[k * BS : (k + 1) * BS, :] = top
        low[k * BS : (k + 1) * BS, :] = (rows - top.astype(jnp.float32)).astype(jnp.bfloat16)


def corner_inverse(corner):
    half = jax.ShapeDtypeStruct((WIDTH, WIDTH), jnp.bfloat16)
    return pl.pallas_call(
        corner_kernel,
        out_shape=(half, half),
        scratch_shapes=[pltpu.VMEM((WIDTH, WIDTH), jnp.float32)],
        compiler_params=pltpu.CompilerParams(vmem_limit_bytes=40 << 20),
        name="corner_inverse",
    )(corner)


def split(value):
    high = value.astype(jnp.bfloat16)
    return high, (value - high.astype(jnp.float32)).astype(jnp.bfloat16)


def wide(left, right, dims):
    return lax.dot_general(left, right, (dims, ((), ())), preferred_element_type=jnp.float32)


NT = ((1,), (1,))
NN = ((1,), (0,))


def product(left, right, dims):
    (lh, ll), (rh, rl) = left, right
    return wide(lh, rh, dims) + wide(lh, rl, dims) + wide(ll, rh, dims)


def update_kernel(grid_rows, grid_cols, place, matrix, high, low, left_raw, *rest):
    ratio = grid_rows // grid_cols
    right_raw, (out, left_high, left_low, right_high, right_low) = rest[:ratio], rest[ratio:]
    own_row, own_col = place[0], place[1]
    i, j = pl.program_id(0), pl.program_id(1)
    tile_rows, tile_cols = out.shape

    @pl.when(i == 0)
    def _():
        for t in range(ratio):
            for b in range(tile_cols // (BS * ratio)):
                raw = split(right_raw[t][0, b * BS : (b + 1) * BS, :])
                at = pl.multiple_of(j * tile_cols + (b * ratio + t) * BS, BS)
                for k in range(PANELS):
                    size = (k + 1) * BS
                    span = slice(k * BS, size)
                    value = product(
                        (high[span, :size], low[span, :size]), (raw[0][:, :size], raw[1][:, :size]), NT
                    )
                    top, rest_ = split(value)
                    right_high[span, pl.ds(at, BS)] = top
                    right_low[span, pl.ds(at, BS)] = rest_

    @pl.when(j == 0)
    def _():
        for b in range(tile_rows // BS):
            at = slice(b * BS, (b + 1) * BS)
            raw = split(left_raw[0, at, :])
            for k in range(PANELS):
                size = (k + 1) * BS
                span = slice(k * BS, size)
                value = product(
                    (raw[0][:, :size], raw[1][:, :size]), (high[span, :size], low[span, :size]), NT
                )
                left_high[at, span], left_low[at, span] = split(value)

    at = pl.ds(pl.multiple_of(j * tile_cols, BS), tile_cols)
    lh, ll = left_high[...], left_low[...]
    rh, rl = right_high[:, at], right_low[:, at]
    out[...] = matrix[...] - product((lh, ll), (rh, rl), NN)

    @pl.when((i == 0) & (own_row < PANELS))
    def _():
        out[:BS, :] = jnp.zeros((BS, tile_cols), jnp.float32)

    @pl.when(j == 0)
    def _():
        for k in range(PANELS):
            @pl.when(own_col == k)
            def _():
                span = slice(k * BS, (k + 1) * BS)
                row = lax.broadcasted_iota(jnp.int32, (tile_rows, BS), 0)
                lane = lax.broadcasted_iota(jnp.int32, (tile_rows, BS), 1)
                block = (i * (tile_rows // BS) + row // BS) * grid_rows + own_row
                kept = (block > k) | ((block == k) & (lane <= lax.rem(row, BS)))
                value = left_high[:, span].astype(jnp.float32) + left_low[:, span].astype(jnp.float32)
                out[:, :BS] = jnp.where(kept, value, 0.0)


def update(grid_rows, grid_cols, own_row, own_col, matrix, high, low, raw):
    rows, cols = matrix.shape
    ratio = grid_rows // grid_cols
    tile_rows, tile_cols = min(512, rows), min(1024, cols)
    last = cols // tile_cols - 1
    slots = [jnp.where(own_row == own_col + grid_cols * t, 0, 1 + t) for t in range(ratio)]
    place = jnp.stack([own_row, own_col, *slots]).astype(jnp.int32)
    whole = pl.BlockSpec((WIDTH, WIDTH), lambda i, j, place: (0, 0))
    tile_spec = pl.BlockSpec((tile_rows, tile_cols), lambda i, j, place: (i, j))
    left_spec = pl.BlockSpec((1, tile_rows, WIDTH), lambda i, j, place: (0, i, 0))
    right_specs = [
        pl.BlockSpec(
            (1, tile_cols // ratio, WIDTH),
            lambda i, j, place, t=t: (place[2 + t], jnp.where(i == 0, j, last), 0),
        )
        for t in range(ratio)
    ]
    half = jnp.bfloat16
    return pl.pallas_call(
        functools.partial(update_kernel, grid_rows, grid_cols),
        out_shape=jax.ShapeDtypeStruct(matrix.shape, jnp.float32),
        grid_spec=pltpu.PrefetchScalarGridSpec(
            num_scalar_prefetch=1,
            grid=(rows // tile_rows, cols // tile_cols),
            in_specs=[tile_spec, whole, whole, left_spec, *right_specs],
            out_specs=tile_spec,
            scratch_shapes=[
                pltpu.VMEM((tile_rows, WIDTH), half),
                pltpu.VMEM((tile_rows, WIDTH), half),
                pltpu.VMEM((WIDTH, cols), half),
                pltpu.VMEM((WIDTH, cols), half),
            ],
        ),
        compiler_params=pltpu.CompilerParams(
            dimension_semantics=("arbitrary", "arbitrary"), vmem_limit_bytes=60 << 20
        ),
        name="update",
    )(place, matrix, high, low, raw, *[raw] * ratio)


def on_device(gram):
    matrix = gram[0, 0]
    grid_rows = lax.axis_size("row")
    grid_cols = lax.axis_size("col")
    assert grid_rows % grid_cols == 0 and grid_cols % CORES == 0 and grid_cols >= PANELS
    raw, corner = exchange(grid_rows, grid_cols, matrix)
    high, low = corner_inverse(corner)
    result = update(
        grid_rows, grid_cols, lax.axis_index("row"), lax.axis_index("col"), matrix, high, low, raw
    )
    return result[None, None]


def solution(mesh):
    in_specs = (P("row", "col", None, None),)
    out_specs = P("row", "col", None, None)
    return jax.shard_map(
        on_device, mesh=mesh, in_specs=in_specs, out_specs=out_specs, check_vma=False
    )
```

```python
import functools

import jax
import jax.numpy as jnp
from jax import lax
from jax.experimental import pallas as pl
from jax.experimental.pallas import tpu as pltpu
from jax.sharding import PartitionSpec as P

BS = 256
PANELS = 3
WIDTH = BS * PANELS
GROUP = 64
CORES = 2
LAG = 2
HI = lax.Precision.HIGHEST
MESH = pl.DeviceIdType.MESH
PAIRS = [(row, col) for col in range(PANELS) for row in range(col, PANELS)]


def lanes(col):
    return jnp.broadcast_to(col, (8, 128))

def eliminate(x, width):
    lane = lax.broadcasted_iota(jnp.int32, (8, 128), 1)
    sub = lax.broadcasted_iota(jnp.int32, (8, 128), 0)
    n = GROUP // 8
    nl = width // 128
    v = [[x[8*r:8*r+8, 128*l:128*l+128] for l in range(nl)] for r in range(n)]
    for r in range(n):
        base = 8 * r
        cols = {q: [lanes(v[q][0][:, base+j:base+j+1]) for j in range(8)] for q in range(r, n)}
        s = {(i, l): lanes(cols[r][l][i:i+1, :]) for i in range(8) for l in range(i, 8)}
        rows = [[lanes(v[r][l][j:j+1, :]) for l in range(nl)] for j in range(8)]
        inv = []
        unit = {}
        mult = {}
        for j in range(8):
            d = s[j, j]
            inv.append(recip(d))
            for i in range(j + 1, 8):
                f = s[j, i] * inv[j]
                mult[i, j] = f
                for l in range(i, 8):
                    s[i, l] = s[i, l] - f * s[j, l]
        for i in range(8):
            for l in range(i):
                t = mult[i, l]
                for m in range(l + 1, i):
                    t = t + mult[i, m] * unit[m, l]
                unit[i, l] = -t
        wcol = []
        for j in range(8):
            t = jnp.where(sub == j, 1.0, 0.0)
            for i in range(j + 1, 8):
                t = jnp.where(sub == i, unit[i, j], t)
            wcol.append(t)
        dvec = s[0, 0]
        for j in range(1, 8):
            dvec = jnp.where(sub == j, s[j, j], dvec)
        scale = lax.rsqrt(dvec)
        ident = [jnp.where((lane >= base) & (lane < base + 8), jnp.where(lane == base + j, 1.0, 0.0), rows[j][0]) for j in range(8)]
        for q in range(r + 1, n):
            c = list(cols[q])
            f = []
            for j in range(8):
                fj = c[j] * inv[j]
                f.append(fj)
                for l in range(j + 1, 8):
                    c[l] = c[l] - fj * s[j, l]
            first = jnp.where((lane >= base) & (lane < base + 8), 0.0, v[q][0])
            acc = [first] + [v[q][l] for l in range(1, nl)]
            for j in range(8):
                g = f[j]
                for i in range(j + 1, 8):
                    g = g + f[i] * unit[i, j]
                acc[0] = acc[0] - g * ident[j]
                for l in range(1, nl):
                    acc[l] = acc[l] - g * rows[j][l]
            v[q] = acc
        new = []
        for l in range(nl):
            t = wcol[0] * (ident[0] if l == 0 else rows[0][l])
            for j in range(1, 8):
                t = t + wcol[j] * (ident[j] if l == 0 else rows[j][l])
            new.append(t * scale)
        upper = wcol[0] * rows[0][0]
        for j in range(1, 8):
            upper = upper + wcol[j] * rows[j][0]
        keep = (lane > base + sub) & (lane < base + 8)
        new[0] = jnp.where(keep, upper * scale, new[0])
        v[r] = new
    return jnp.concatenate([jnp.concatenate(t, axis=1) for t in v], axis=0)

def recip(d):
    r = pl.reciprocal(d, approx=True)
    r = r * (2.0 - d * r)
    return r

def factor(m, bs, panels, hook=None):
    width = bs * panels
    groups = bs // GROUP
    for k in range(panels):
        def body(g, carry):
            start = pl.multiple_of(k * bs + g * GROUP, GROUP)
            rows = m[pl.ds(start, GROUP), :]
            x = pltpu.roll(rows, width - start, axis=1)
            x = eliminate(x, width)
            x = pltpu.roll(x, start, axis=1)
            m[pl.ds(start, GROUP), :] = x
            lane = lax.broadcasted_iota(jnp.int32, (GROUP, width), 1)
            sub = lax.broadcasted_iota(jnp.int32, (GROUP, width), 0)
            upd = jnp.where((lane - start > sub) & (lane < start + GROUP), 0.0, x)
            own = x[:, k*bs:(k+1)*bs]
            lane_own = lax.broadcasted_iota(jnp.int32, (GROUP, bs), 1) + k * bs
            left = jnp.where(lane_own >= start + GROUP, own, 0.0)
            prod = lax.dot_general(left, upd, (((0,), (0,)), ((), ())), precision=HI, preferred_element_type=jnp.float32)
            old = m[k*bs:(k+1)*bs, :]
            r2 = lax.broadcasted_iota(jnp.int32, (bs, width), 0) + k * bs
            l2 = lax.broadcasted_iota(jnp.int32, (bs, width), 1)
            old = jnp.where((r2 >= start + GROUP) & (l2 >= start) & (l2 < start + GROUP), 0.0, old)
            m[k*bs:(k+1)*bs, :] = old - prod
            if hook is not None: hook(k * groups + g)
            return carry
        lax.fori_loop(0, groups, body, 0)
        if k + 1 < panels:
            full = m[k*bs:(k+1)*bs, :]
            l2 = lax.broadcasted_iota(jnp.int32, (bs, width), 1)
            r2 = lax.broadcasted_iota(jnp.int32, (bs, width), 0) + k * bs
            upd = jnp.where((l2 > r2) & (l2 < (k+1)*bs), 0.0, full)
            for r in range(k + 1, panels):
                left = m[k*bs:(k+1)*bs, r*bs:(r+1)*bs]
                prod = lax.dot_general(left, upd, (((0,), (0,)), ((), ())), precision=HI, preferred_element_type=jnp.float32)
                if k > 0:
                    m[r*bs:(r+1)*bs, :k*bs] -= prod[:, :k*bs]
                m[r*bs:(r+1)*bs, k*bs:(k+1)*bs] = -prod[:, k*bs:(k+1)*bs]
                m[r*bs:(r+1)*bs, (k+1)*bs:] -= prod[:, (k+1)*bs:]

def exchange_kernel(
    grid_rows, grid_cols, blocks, matrix, raw, high, low,
    stage, spare, corner, m, stage_sem, scatter_send, fan_send, core_send, corner_recv,
    left_send, left_recv, right_send, right_recv, spare_send, spare_recv,
):
    own_row, own_col = lax.axis_index("row"), lax.axis_index("col")
    ratio = grid_rows // grid_cols
    core = lax.rem(own_row, CORES)
    plane, planes = own_row // CORES, grid_rows // CORES
    steps = blocks * PANELS
    has_up, has_down = plane + 1 < planes, plane > 0
    up = jnp.minimum(own_row + CORES, grid_rows - CORES + core)
    down = jnp.maximum(own_row - CORES, core)
    partner = own_row + 1 - 2 * core

    def beside(other):
        return lax.rem(own_col + other, grid_cols)

    barrier = pltpu.get_barrier_semaphore()
    for other in range(1, grid_cols):
        pl.semaphore_signal(barrier, inc=1, device_id=(own_row, beside(other)), device_id_type=MESH)
    pl.semaphore_signal(barrier, inc=1, device_id=(partner, own_col), device_id_type=MESH)

    @pl.when(has_up)
    def _():
        pl.semaphore_signal(barrier, inc=1, device_id=(up, own_col), device_id_type=MESH)

    @pl.when(has_down)
    def _():
        pl.semaphore_signal(barrier, inc=1, device_id=(down, own_col), device_id_type=MESH)

    pl.semaphore_wait(barrier, grid_cols + has_up.astype(jnp.int32) + has_down.astype(jnp.int32))

    def copy(src, dst, send, recv, row, col):
        return pltpu.make_async_remote_copy(
            src_ref=src, dst_ref=dst, send_sem=send, recv_sem=recv,
            device_id=(row, col), device_id_type=MESH,
        )

    fetch = pltpu.make_async_copy(matrix.at[:, 0:BS], stage, stage_sem)

    @pl.when(own_col < PANELS)
    def _():
        fetch.start()

    size = BS // grid_cols

    def part_of(n, j):
        span = pl.ds(pl.multiple_of(j * size, 8), size)
        return span, corner.at[n, span], corner_recv.at[n, j]

    def scatter(act):
        for n, (row, col) in enumerate(PAIRS):
            @pl.when((own_row == row) & (own_col == col))
            def _():
                for other in range(1, grid_cols):
                    j = beside(other)
                    span, here, recv = part_of(n, j)
                    act(copy(matrix.at[span, 0:BS], here, scatter_send.at[other], recv, own_row, j))

    def on_line(n, act, wait):
        row, col = PAIRS[n]

        @pl.when(core == row % CORES)
        def _():
            span, here, recv = part_of(n, own_col)
            source = (own_row == row) & (own_col == col)

            def fan(src):
                @pl.when(has_up & (own_row >= row))
                def _():
                    act(copy(src, here, fan_send.at[n, 0], recv, up, own_col))

                @pl.when(has_down & (own_row <= row))
                def _():
                    act(copy(src, here, fan_send.at[n, grid_cols], recv, down, own_col))

                for other in range(1, grid_cols):
                    act(copy(src, here, fan_send.at[n, other], recv, own_row, beside(other)))
                act(copy(src, here, core_send.at[n, own_col], recv, partner, own_col))

            @pl.when(source)
            def _():
                fan(matrix.at[span, 0:BS])

            @pl.when(jnp.logical_not(source))
            def _():
                if wait:
                    copy(here, here, core_send.at[n, own_col], recv, partner, own_col).wait_recv()
                fan(here)

    def off_line(n, act, wait):
        primary = core == PAIRS[n][0] % CORES

        def one(j, carry):
            span, here, recv = part_of(n, j)
            c = copy(here, here, core_send.at[n, j], recv, partner, own_col)

            @pl.when((j != own_col) | jnp.logical_not(primary))
            def _():
                if wait:
                    c.wait_recv()

                @pl.when(primary)
                def _():
                    act(c)
            return carry

        lax.fori_loop(0, grid_cols, one, 0)

    def start(c):
        c.start()

    def end(c):
        c.wait_send()

    scatter(start)
    for n in range(len(PAIRS)):
        on_line(n, start, True)

    root_col = lax.rem(own_row, grid_cols)
    spare_col = lax.rem(root_col + grid_cols // 2, grid_cols)

    def tile(slot, i, k):
        return raw.at[slot, pl.ds(pl.multiple_of(i * BS, BS), BS), pl.ds(pl.multiple_of(k * BS, BS), BS)]

    def each_left(act):
        second = grid_cols // 2
        order = [[0, second], *[[o] for o in range(1, grid_cols) if o != second]]
        for others in order:
            def one(i, carry):
                for other in others:
                    col = lax.rem(root_col + other, grid_cols)
                    for k in range(PANELS):
                        @pl.when((own_col == k) & (col != own_col))
                        def _():
                            act(copy(
                                stage.at[pl.ds(pl.multiple_of(i * BS, BS), BS)], tile(0, i, k),
                                left_send.at[other, i], left_recv.at[i * PANELS + k], own_row, col,
                            ))
                return carry
            lax.fori_loop(0, blocks, one, 0)

    @pl.when(own_col < PANELS)
    def _():
        fetch.wait()

    each_left(start)

    for n, (row, col) in enumerate(PAIRS):
        @pl.when((own_row == row) & (own_col == col))
        def _():
            span, here, recv = part_of(n, own_col)
            keep = pltpu.make_async_copy(stage.at[span], here, stage_sem)
            keep.start()
            keep.wait()
    for k in range(PANELS):
        @pl.when(own_col == k)
        def _():
            pltpu.make_async_copy(stage, raw.at[0, :, k * BS : (k + 1) * BS], stage_sem).start()

    for n in range(len(PAIRS)):
        off_line(n, start, True)

    active = core == lax.rem(own_col, CORES)
    divert = ratio > 1 and planes > CORES
    spare_step = jnp.minimum(spare_col, PANELS - 1)
    into_end = jnp.where(plane == 1, down, up)
    is_source = (own_col == spare_col) & ((plane == 1) | (plane == planes - 2))
    from_row = jnp.where(plane == 0, up, down)
    is_spare = (own_col == lax.rem(from_row + grid_cols // 2, grid_cols)) & ((plane == 0) | (plane == planes - 1))
    home = lax.rem(from_row, grid_cols)

    def need_left(step):
        k = lax.rem(step, PANELS)

        @pl.when(own_col != k)
        def _():
            here = tile(0, step // PANELS, k)
            copy(here, here, left_send.at[0, 0], left_recv.at[step], partner, own_col).wait_recv()

        @pl.when((own_col == k) & (step == k))
        def _():
            pltpu.make_async_copy(stage, raw.at[0, :, 0:BS], stage_sem).wait()

    def right(turn, act, wait):
        is_root = own_col == root_col
        if wait:
            @pl.when(is_root & (turn < steps))
            def _():
                need_left(turn)
        if divert:
            i, k = turn // PANELS, lax.rem(turn, PANELS)

            @pl.when(is_source & (turn < steps) & (k == spare_step))
            def _():
                if wait:
                    need_left(turn)
                act(copy(tile(0, i, k), spare.at[i], spare_send.at[i], spare_recv.at[i], into_end, own_col))

            late = turn - LAG
            i, k = late // PANELS, lax.rem(late, PANELS)

            @pl.when(is_spare & (late >= 0) & (late < steps) & (k == jnp.minimum(own_col, PANELS - 1)))
            def _():
                here = spare.at[i]
                if wait:
                    copy(here, here, spare_send.at[i], spare_recv.at[i], partner, own_col).wait_recv()
                slot = from_row // grid_cols
                for t in range(ratio):
                    @pl.when(slot == t)
                    def _():
                        act(copy(here, tile(1 + t, i, k), spare_send.at[i], right_recv.at[t, late], own_row, home))
        for t in range(ratio):
            source = own_col + grid_cols * t
            root = own_row == source
            level = source // CORES
            step = turn - LAG * jnp.abs(plane - level)

            @pl.when((step >= 0) & (step < steps))
            def _():
                i, k = step // PANELS, lax.rem(step, PANELS)
                here = tile(1 + t, i, k)

                def send(src, index, to_row):
                    act(copy(
                        src, here, right_send.at[t, index, step], right_recv.at[t, step], to_row, own_col
                    ))

                def fan(src, go_up, go_down):
                    @pl.when(go_up)
                    def _():
                        send(src, 0, up)

                    @pl.when(go_down)
                    def _():
                        send(src, 1, down)

                    send(src, 2, partner)

                @pl.when(root)
                def _():
                    if divert:
                        other = k == spare_step
                        fan(
                            tile(0, i, k),
                            has_up & jnp.logical_not(other & (plane != 1) & (plane == planes - 2)),
                            has_down & jnp.logical_not(other & (plane == 1)),
                        )
                    else:
                        fan(tile(0, i, k), has_up, has_down)

                @pl.when(jnp.logical_not(root))
                def _():
                    if wait:
                        copy(
                            here, here, right_send.at[t, 2, step], right_recv.at[t, step], partner, own_col
                        ).wait_recv()

                    @pl.when(active)
                    def _():
                        fan(here, has_up & (own_row > source), has_down & (own_row < source))

    turns = steps + LAG * (planes - 1)

    def go(turn, carry):
        right(turn, start, True)
        return carry

    def finish(turn, carry):
        right(turn, end, False)
        return carry

    for n, (row, col) in enumerate(PAIRS):
        block = corner[n]
        m[col * BS : (col + 1) * BS, row * BS : (row + 1) * BS] = block.T
        if row != col:
            m[row * BS : (row + 1) * BS, col * BS : (col + 1) * BS] = block
    factor(m, BS, PANELS, lambda index: right(index, start, True))
    for k in range(PANELS):
        rows = m[k * BS : (k + 1) * BS, :]
        lane = lax.broadcasted_iota(jnp.int32, rows.shape, 1)
        sub = lax.broadcasted_iota(jnp.int32, rows.shape, 0) + k * BS
        rows = jnp.where(lane > sub, 0.0, rows)
        top = rows.astype(jnp.bfloat16)
        high[k * BS : (k + 1) * BS, :] = top
        low[k * BS : (k + 1) * BS, :] = (rows - top.astype(jnp.float32)).astype(jnp.bfloat16)

    lax.fori_loop(PANELS * (BS // GROUP), turns, go, 0)

    def rest(step, carry):
        k = lax.rem(step, PANELS)
        done = own_col == root_col
        if divert:
            done = done | (is_source & (k == spare_step))

        @pl.when(jnp.logical_not(done))
        def _():
            need_left(step)
        return carry

    lax.fori_loop(0, steps, rest, 0)
    lax.fori_loop(0, turns, finish, 0)
    each_left(end)
    scatter(end)
    for n in range(len(PAIRS)):
        on_line(n, end, False)
        off_line(n, end, False)


def exchange(grid_rows, grid_cols, matrix):
    rows = matrix.shape[0]
    blocks = rows // BS
    ratio = grid_rows // grid_cols
    steps = blocks * PANELS
    tiles = len(PAIRS)
    dma = pltpu.SemaphoreType.DMA
    half = jax.ShapeDtypeStruct((WIDTH, WIDTH), jnp.bfloat16)
    in_hbm, in_vmem = pl.BlockSpec(memory_space=pltpu.HBM), pl.BlockSpec(memory_space=pltpu.VMEM)
    return pl.pallas_call(
        functools.partial(exchange_kernel, grid_rows, grid_cols, blocks),
        out_shape=(jax.ShapeDtypeStruct((1 + ratio, rows, WIDTH), jnp.float32), half, half),
        in_specs=[in_hbm],
        out_specs=(in_hbm, in_vmem, in_vmem),
        scratch_shapes=[
            pltpu.VMEM((rows, BS), jnp.float32),
            pltpu.VMEM((blocks, BS, BS), jnp.float32),
            pltpu.VMEM((tiles, BS, BS), jnp.float32),
            pltpu.VMEM((WIDTH, WIDTH), jnp.float32),
            dma,
            dma((grid_cols,)),
            dma((tiles, 1 + grid_cols)),
            dma((tiles, grid_cols)),
            dma((tiles, grid_cols)),
            dma((grid_cols, blocks)),
            dma((steps,)),
            dma((ratio, 3, steps)),
            dma((ratio, steps)),
            dma((blocks,)),
            dma((blocks,)),
        ],
        compiler_params=pltpu.CompilerParams(
            collective_id=0, has_side_effects=True, vmem_limit_bytes=40 << 20
        ),
        name="exchange",
    )(matrix)


def split(value):
    high = value.astype(jnp.bfloat16)
    return high, (value - high.astype(jnp.float32)).astype(jnp.bfloat16)


def wide(left, right, dims):
    return lax.dot_general(left, right, (dims, ((), ())), preferred_element_type=jnp.float32)


NT = ((1,), (1,))
NN = ((1,), (0,))


def product(left, right, dims):
    (lh, ll), (rh, rl) = left, right
    return wide(lh, rh, dims) + wide(lh, rl, dims) + wide(ll, rh, dims)


def update_kernel(grid_rows, grid_cols, place, matrix, high, low, left_raw, *rest):
    ratio = grid_rows // grid_cols
    right_raw, (out, left_high, left_low, right_high, right_low) = rest[:ratio], rest[ratio:]
    own_row, own_col = place[0], place[1]
    i, j = pl.program_id(0), pl.program_id(1)
    tile_rows, tile_cols = out.shape

    @pl.when(i == 0)
    def _():
        for t in range(ratio):
            for b in range(tile_cols // (BS * ratio)):
                raw = split(right_raw[t][0, b * BS : (b + 1) * BS, :])
                at = pl.multiple_of(j * tile_cols + (b * ratio + t) * BS, BS)
                for k in range(PANELS):
                    size = (k + 1) * BS
                    span = slice(k * BS, size)
                    value = product(
                        (high[span, :size], low[span, :size]), (raw[0][:, :size], raw[1][:, :size]), NT
                    )
                    top, rest_ = split(value)
                    right_high[span, pl.ds(at, BS)] = top
                    right_low[span, pl.ds(at, BS)] = rest_

    @pl.when(j == 0)
    def _():
        for b in range(tile_rows // BS):
            at = slice(b * BS, (b + 1) * BS)
            raw = split(left_raw[0, at, :])
            for k in range(PANELS):
                size = (k + 1) * BS
                span = slice(k * BS, size)
                value = product(
                    (raw[0][:, :size], raw[1][:, :size]), (high[span, :size], low[span, :size]), NT
                )
                left_high[at, span], left_low[at, span] = split(value)

    at = pl.ds(pl.multiple_of(j * tile_cols, BS), tile_cols)
    lh, ll = left_high[...], left_low[...]
    rh, rl = right_high[:, at], right_low[:, at]
    out[...] = matrix[...] - product((lh, ll), (rh, rl), NN)

    @pl.when((i == 0) & (own_row < PANELS))
    def _():
        out[:BS, :] = jnp.zeros((BS, tile_cols), jnp.float32)

    @pl.when(j == 0)
    def _():
        for k in range(PANELS):
            @pl.when(own_col == k)
            def _():
                span = slice(k * BS, (k + 1) * BS)
                row = lax.broadcasted_iota(jnp.int32, (tile_rows, BS), 0)
                lane = lax.broadcasted_iota(jnp.int32, (tile_rows, BS), 1)
                block = (i * (tile_rows // BS) + row // BS) * grid_rows + own_row
                kept = (block > k) | ((block == k) & (lane <= lax.rem(row, BS)))
                value = left_high[:, span].astype(jnp.float32) + left_low[:, span].astype(jnp.float32)
                out[:, :BS] = jnp.where(kept, value, 0.0)


def update(grid_rows, grid_cols, own_row, own_col, matrix, high, low, raw):
    rows, cols = matrix.shape
    ratio = grid_rows // grid_cols
    tile_rows, tile_cols = min(512, rows), min(1024, cols)
    last = cols // tile_cols - 1
    slots = [jnp.where(own_row == own_col + grid_cols * t, 0, 1 + t) for t in range(ratio)]
    place = jnp.stack([own_row, own_col, *slots]).astype(jnp.int32)
    whole = pl.BlockSpec((WIDTH, WIDTH), lambda i, j, place: (0, 0))
    tile_spec = pl.BlockSpec((tile_rows, tile_cols), lambda i, j, place: (i, j))
    left_spec = pl.BlockSpec((1, tile_rows, WIDTH), lambda i, j, place: (0, i, 0))
    right_specs = [
        pl.BlockSpec(
            (1, tile_cols // ratio, WIDTH),
            lambda i, j, place, t=t: (place[2 + t], jnp.where(i == 0, j, last), 0),
        )
        for t in range(ratio)
    ]
    half = jnp.bfloat16
    return pl.pallas_call(
        functools.partial(update_kernel, grid_rows, grid_cols),
        out_shape=jax.ShapeDtypeStruct(matrix.shape, jnp.float32),
        grid_spec=pltpu.PrefetchScalarGridSpec(
            num_scalar_prefetch=1,
            grid=(rows // tile_rows, cols // tile_cols),
            in_specs=[tile_spec, whole, whole, left_spec, *right_specs],
            out_specs=tile_spec,
            scratch_shapes=[
                pltpu.VMEM((tile_rows, WIDTH), half),
                pltpu.VMEM((tile_rows, WIDTH), half),
                pltpu.VMEM((WIDTH, cols), half),
                pltpu.VMEM((WIDTH, cols), half),
            ],
        ),
        compiler_params=pltpu.CompilerParams(
            dimension_semantics=("arbitrary", "arbitrary"), vmem_limit_bytes=60 << 20
        ),
        name="update",
    )(place, matrix, high, low, raw, *[raw] * ratio)


def on_device(gram):
    matrix = gram[0, 0]
    grid_rows = lax.axis_size("row")
    grid_cols = lax.axis_size("col")
    assert grid_rows % grid_cols == 0 and grid_cols % CORES == 0 and grid_cols >= PANELS
    raw, high, low = exchange(grid_rows, grid_cols, matrix)
    result = update(
        grid_rows, grid_cols, lax.axis_index("row"), lax.axis_index("col"), matrix, high, low, raw
    )
    return result[None, None]


def solution(mesh):
    in_specs = (P("row", "col", None, None),)
    out_specs = P("row", "col", None, None)
    return jax.shard_map(
        on_device, mesh=mesh, in_specs=in_specs, out_specs=out_specs, check_vma=False
    )
```

```python
import functools

import jax
import jax.numpy as jnp
from jax import lax
from jax.experimental import pallas as pl
from jax.experimental.pallas import tpu as pltpu
from jax.sharding import PartitionSpec as P

BS = 256
PANELS = 3
WIDTH = BS * PANELS
GROUP = 64
CORES = 2
LAG = 3
AHEAD = 2
HI = lax.Precision.HIGHEST
MESH = pl.DeviceIdType.MESH
PAIRS = [(row, col) for col in range(PANELS) for row in range(col, PANELS)]


def lanes(col):
    return jnp.broadcast_to(col, (8, 128))

def eliminate(x, width):
    lane = lax.broadcasted_iota(jnp.int32, (8, 128), 1)
    sub = lax.broadcasted_iota(jnp.int32, (8, 128), 0)
    n = GROUP // 8
    nl = width // 128
    v = [[x[8*r:8*r+8, 128*l:128*l+128] for l in range(nl)] for r in range(n)]
    for r in range(n):
        base = 8 * r
        cols = {q: [lanes(v[q][0][:, base+j:base+j+1]) for j in range(8)] for q in range(r, n)}
        s = {(i, l): lanes(cols[r][l][i:i+1, :]) for i in range(8) for l in range(i, 8)}
        rows = [[lanes(v[r][l][j:j+1, :]) for l in range(nl)] for j in range(8)]
        inv = []
        unit = {}
        mult = {}
        for j in range(8):
            d = s[j, j]
            inv.append(recip(d))
            for i in range(j + 1, 8):
                f = s[j, i] * inv[j]
                mult[i, j] = f
                for l in range(i, 8):
                    s[i, l] = s[i, l] - f * s[j, l]
        for i in range(8):
            for l in range(i):
                t = mult[i, l]
                for m in range(l + 1, i):
                    t = t + mult[i, m] * unit[m, l]
                unit[i, l] = -t
        wcol = []
        for j in range(8):
            t = jnp.where(sub == j, 1.0, 0.0)
            for i in range(j + 1, 8):
                t = jnp.where(sub == i, unit[i, j], t)
            wcol.append(t)
        dvec = s[0, 0]
        for j in range(1, 8):
            dvec = jnp.where(sub == j, s[j, j], dvec)
        scale = lax.rsqrt(dvec)
        ident = [jnp.where((lane >= base) & (lane < base + 8), jnp.where(lane == base + j, 1.0, 0.0), rows[j][0]) for j in range(8)]
        for q in range(r + 1, n):
            c = list(cols[q])
            f = []
            for j in range(8):
                fj = c[j] * inv[j]
                f.append(fj)
                for l in range(j + 1, 8):
                    c[l] = c[l] - fj * s[j, l]
            first = jnp.where((lane >= base) & (lane < base + 8), 0.0, v[q][0])
            acc = [first] + [v[q][l] for l in range(1, nl)]
            for j in range(8):
                g = f[j]
                for i in range(j + 1, 8):
                    g = g + f[i] * unit[i, j]
                acc[0] = acc[0] - g * ident[j]
                for l in range(1, nl):
                    acc[l] = acc[l] - g * rows[j][l]
            v[q] = acc
        new = []
        for l in range(nl):
            t = wcol[0] * (ident[0] if l == 0 else rows[0][l])
            for j in range(1, 8):
                t = t + wcol[j] * (ident[j] if l == 0 else rows[j][l])
            new.append(t * scale)
        upper = wcol[0] * rows[0][0]
        for j in range(1, 8):
            upper = upper + wcol[j] * rows[j][0]
        keep = (lane > base + sub) & (lane < base + 8)
        new[0] = jnp.where(keep, upper * scale, new[0])
        v[r] = new
    return jnp.concatenate([jnp.concatenate(t, axis=1) for t in v], axis=0)

def recip(d):
    r = pl.reciprocal(d, approx=True)
    r = r * (2.0 - d * r)
    return r

def factor(m, bs, panels, hook=None):
    width = bs * panels
    groups = bs // GROUP
    for k in range(panels):
        def body(g, carry):
            start = pl.multiple_of(k * bs + g * GROUP, GROUP)
            rows = m[pl.ds(start, GROUP), :]
            x = pltpu.roll(rows, width - start, axis=1)
            x = eliminate(x, width)
            x = pltpu.roll(x, start, axis=1)
            m[pl.ds(start, GROUP), :] = x
            lane = lax.broadcasted_iota(jnp.int32, (GROUP, width), 1)
            sub = lax.broadcasted_iota(jnp.int32, (GROUP, width), 0)
            upd = jnp.where((lane - start > sub) & (lane < start + GROUP), 0.0, x)
            own = x[:, k*bs:(k+1)*bs]
            lane_own = lax.broadcasted_iota(jnp.int32, (GROUP, bs), 1) + k * bs
            left = jnp.where(lane_own >= start + GROUP, own, 0.0)
            prod = lax.dot_general(left, upd, (((0,), (0,)), ((), ())), precision=HI, preferred_element_type=jnp.float32)
            old = m[k*bs:(k+1)*bs, :]
            r2 = lax.broadcasted_iota(jnp.int32, (bs, width), 0) + k * bs
            l2 = lax.broadcasted_iota(jnp.int32, (bs, width), 1)
            old = jnp.where((r2 >= start + GROUP) & (l2 >= start) & (l2 < start + GROUP), 0.0, old)
            m[k*bs:(k+1)*bs, :] = old - prod
            if hook is not None: hook(k * groups + g)
            return carry
        lax.fori_loop(0, groups, body, 0)
        if k + 1 < panels:
            full = m[k*bs:(k+1)*bs, :]
            l2 = lax.broadcasted_iota(jnp.int32, (bs, width), 1)
            r2 = lax.broadcasted_iota(jnp.int32, (bs, width), 0) + k * bs
            upd = jnp.where((l2 > r2) & (l2 < (k+1)*bs), 0.0, full)
            for r in range(k + 1, panels):
                left = m[k*bs:(k+1)*bs, r*bs:(r+1)*bs]
                prod = lax.dot_general(left, upd, (((0,), (0,)), ((), ())), precision=HI, preferred_element_type=jnp.float32)
                if k > 0:
                    m[r*bs:(r+1)*bs, :k*bs] -= prod[:, :k*bs]
                m[r*bs:(r+1)*bs, k*bs:(k+1)*bs] = -prod[:, k*bs:(k+1)*bs]
                m[r*bs:(r+1)*bs, (k+1)*bs:] -= prod[:, (k+1)*bs:]

def split(value):
    high = value.astype(jnp.bfloat16)
    return high, (value - high.astype(jnp.float32)).astype(jnp.bfloat16)


def wide(left, right, dims):
    return lax.dot_general(left, right, (dims, ((), ())), preferred_element_type=jnp.float32)


NT = ((1,), (1,))
NN = ((1,), (0,))


def product(left, right, dims):
    (lh, ll), (rh, rl) = left, right
    return wide(lh, rh, dims) + wide(lh, rl, dims) + wide(ll, rh, dims)


def exchange_kernel(
    grid_rows, grid_cols, blocks, done, matrix, part, left_high_out, left_low_out, right_high_out, right_low_out,
    raw, high, low, left_high, left_low, right_high, right_low, tail_high, tail_low, tiles_in, tiles_out,
    spare, corner, m, stage_sem, scatter_send, fan_send, core_send, corner_recv,
    left_send, left_recv, right_send, right_recv, spare_send, spare_recv, strip_keep, strip_send, in_sem, out_sem, left_out_sem, right_out_sem,
):
    own_row, own_col = lax.axis_index("row"), lax.axis_index("col")
    ratio = grid_rows // grid_cols
    core = lax.rem(own_row, CORES)
    plane, planes = own_row // CORES, grid_rows // CORES
    steps = blocks * PANELS
    has_up, has_down = plane + 1 < planes, plane > 0
    up = jnp.minimum(own_row + CORES, grid_rows - CORES + core)
    down = jnp.maximum(own_row - CORES, core)
    partner = own_row + 1 - 2 * core

    def beside(other):
        return lax.rem(own_col + other, grid_cols)

    barrier = pltpu.get_barrier_semaphore()
    for other in range(1, grid_cols):
        pl.semaphore_signal(barrier, inc=1, device_id=(own_row, beside(other)), device_id_type=MESH)
    pl.semaphore_signal(barrier, inc=1, device_id=(partner, own_col), device_id_type=MESH)

    @pl.when(has_up)
    def _():
        pl.semaphore_signal(barrier, inc=1, device_id=(up, own_col), device_id_type=MESH)

    @pl.when(has_down)
    def _():
        pl.semaphore_signal(barrier, inc=1, device_id=(down, own_col), device_id_type=MESH)

    pl.semaphore_wait(barrier, grid_cols + has_up.astype(jnp.int32) + has_down.astype(jnp.int32))

    def copy(src, dst, send, recv, row, col):
        return pltpu.make_async_remote_copy(
            src_ref=src, dst_ref=dst, send_sem=send, recv_sem=recv,
            device_id=(row, col), device_id_type=MESH,
        )

    for k in range(PANELS):
        @pl.when(own_col == k)
        def _():
            pltpu.make_async_copy(matrix.at[:, 0:BS], raw.at[0, :, k * BS : (k + 1) * BS], stage_sem).start()

    size = BS // grid_cols

    def part_of(n, j):
        span = pl.ds(pl.multiple_of(j * size, 8), size)
        return span, corner.at[n, span], corner_recv.at[n, j]

    def scatter(act):
        for n, (row, col) in enumerate(PAIRS):
            @pl.when((own_row == row) & (own_col == col))
            def _():
                for other in range(1, grid_cols):
                    j = beside(other)
                    span, here, recv = part_of(n, j)
                    act(copy(matrix.at[span, 0:BS], here, scatter_send.at[other], recv, own_row, j))

    def on_line(n, act, wait):
        row, col = PAIRS[n]

        @pl.when(core == row % CORES)
        def _():
            span, here, recv = part_of(n, own_col)
            source = (own_row == row) & (own_col == col)

            def fan(src):
                @pl.when(has_up & (own_row >= row))
                def _():
                    act(copy(src, here, fan_send.at[n, 0], recv, up, own_col))

                @pl.when(has_down & (own_row <= row))
                def _():
                    act(copy(src, here, fan_send.at[n, grid_cols], recv, down, own_col))

                for other in range(1, grid_cols):
                    act(copy(src, here, fan_send.at[n, other], recv, own_row, beside(other)))
                act(copy(src, here, core_send.at[n, own_col], recv, partner, own_col))

            @pl.when(source)
            def _():
                fan(matrix.at[span, 0:BS])

            @pl.when(jnp.logical_not(source))
            def _():
                if wait:
                    copy(here, here, core_send.at[n, own_col], recv, partner, own_col).wait_recv()
                fan(here)

    def off_line(n, act, wait):
        primary = core == PAIRS[n][0] % CORES

        def one(j, carry):
            span, here, recv = part_of(n, j)
            c = copy(here, here, core_send.at[n, j], recv, partner, own_col)

            @pl.when((j != own_col) | jnp.logical_not(primary))
            def _():
                if wait:
                    c.wait_recv()

                @pl.when(primary)
                def _():
                    act(c)
            return carry

        lax.fori_loop(0, grid_cols, one, 0)

    def start(c):
        c.start()

    def end(c):
        c.wait_send()

    root_col = lax.rem(own_row, grid_cols)
    spare_col = lax.rem(root_col + grid_cols // 2, grid_cols)

    def tile(slot, i, k):
        return raw.at[slot, pl.ds(pl.multiple_of(i * BS, BS), BS), pl.ds(pl.multiple_of(k * BS, BS), BS)]

    def each_left(act, first, last):
        def one(i, carry):
            for other in range(grid_cols):
                col = lax.rem(root_col + other, grid_cols)
                for k in range(PANELS):
                    @pl.when((own_col == k) & (col != own_col))
                    def _():
                        here = tile(0, i, k)
                        act(copy(here, here, left_send.at[other, i], left_recv.at[i * PANELS + k], own_row, col))
            return carry
        lax.fori_loop(first, last, one, 0)

    scatter(start)

    @pl.when(own_col < PANELS)
    def _():
        pltpu.make_async_copy(matrix.at[:, 0:BS], raw.at[0, :, 0:BS], stage_sem).wait()

    each_left(start, 0, 1)
    for n in range(len(PAIRS)):
        on_line(n, start, True)
    each_left(start, 1, blocks)

    def each_strip(keep, act):
        def one(i, carry):
            for k in range(CORES):
                @pl.when(own_row == k)
                def _():
                    for t in range(ratio):
                        c = pl.multiple_of((t + i * ratio) * BS, BS)
                        src, here = matrix.at[0:BS, pl.ds(c, BS)], tile(1 + t, i, k)

                        @pl.when(own_row != own_col + grid_cols * t)
                        def _():
                            if keep is not None:
                                keep(pltpu.make_async_copy(src, here, strip_keep.at[t, i]))

                        @pl.when(partner != own_col + grid_cols * t)
                        def _():
                            act(copy(
                                src, here, strip_send.at[t, i], right_recv.at[t, i * PANELS + k], partner, own_col
                            ))
            return carry
        lax.fori_loop(0, blocks, one, 0)

    each_strip(start, start)

    for n, (row, col) in enumerate(PAIRS):
        @pl.when((own_row == row) & (own_col == col))
        def _():
            span, here, recv = part_of(n, own_col)
            keep = pltpu.make_async_copy(matrix.at[span, 0:BS], here, stage_sem)
            keep.start()
            keep.wait()


    active = core == lax.rem(own_col, CORES)
    divert = ratio > 1 and planes > CORES
    spare_step = jnp.minimum(spare_col, PANELS - 1)
    is_source = (own_col == spare_col) & (plane == planes - 2)
    is_spare = (own_col == lax.rem(down + grid_cols // 2, grid_cols)) & (plane == planes - 1)
    home = lax.rem(down, grid_cols)

    is_root = own_col == root_col
    first_left = AHEAD + PANELS * (BS // GROUP) + 1

    def early(step):
        passed_on = is_root
        if divert:
            passed_on = passed_on | (is_source & (lax.rem(step, PANELS) == spare_step))
        return passed_on & (step <= first_left + step // PANELS)

    def need_left(step):
        k = lax.rem(step, PANELS)

        @pl.when(own_col != k)
        def _():
            here = tile(0, step // PANELS, k)
            copy(here, here, left_send.at[0, 0], left_recv.at[step], partner, own_col).wait_recv()

    def right(turn, act, wait):
        if wait:
            @pl.when((turn < steps) & early(turn))
            def _():
                need_left(turn)
        if divert:
            i, k = turn // PANELS, lax.rem(turn, PANELS)

            @pl.when(is_source & (turn < steps) & (k == spare_step))
            def _():
                act(copy(tile(0, i, k), spare.at[i], spare_send.at[i], spare_recv.at[i], up, own_col))

            late = turn - LAG
            i, k = late // PANELS, lax.rem(late, PANELS)

            @pl.when(is_spare & (late >= 0) & (late < steps) & (k == jnp.minimum(own_col, PANELS - 1)))
            def _():
                here = spare.at[i]
                if wait:
                    copy(here, here, spare_send.at[i], spare_recv.at[i], partner, own_col).wait_recv()
                slot = down // grid_cols
                for t in range(ratio):
                    @pl.when(slot == t)
                    def _():
                        act(copy(here, tile(1 + t, i, k), spare_send.at[i], right_recv.at[t, late], own_row, home))
        for t in range(ratio):
            source = own_col + grid_cols * t
            root = own_row == source
            level = source // CORES
            step = turn - LAG * jnp.abs(plane - level)

            @pl.when((step >= 0) & (step < steps))
            def _():
                i, k = step // PANELS, lax.rem(step, PANELS)
                here = tile(1 + t, i, k)

                def send(src, index, to_row):
                    act(copy(
                        src, here, right_send.at[t, index, step], right_recv.at[t, step], to_row, own_col
                    ))

                def fan(src, go_up, go_down):
                    @pl.when(go_up)
                    def _():
                        send(src, 0, up)

                    @pl.when(go_down)
                    def _():
                        send(src, 1, down)

                    @pl.when((plane > 0) | (k >= CORES))
                    def _():
                        send(src, 2, partner)

                strips = (plane == 0) & (k < CORES)
                go_down = (plane > 1) | ((plane == 1) & (k >= CORES))

                @pl.when(root)
                def _():
                    go_up = has_up
                    if divert:
                        go_up = has_up & jnp.logical_not((k == spare_step) & (plane == planes - 2))
                    fan(tile(0, i, k), go_up, go_down)

                @pl.when(jnp.logical_not(root))
                def _():
                    if wait:
                        local = strips & (k == own_row)

                        @pl.when(local)
                        def _():
                            pltpu.make_async_copy(here, here, strip_keep.at[t, i]).wait()

                        @pl.when(jnp.logical_not(local))
                        def _():
                            copy(
                                here, here, right_send.at[t, 2, step], right_recv.at[t, step], partner, own_col
                            ).wait_recv()

                    @pl.when(active)
                    def _():
                        fan(here, has_up & (own_row > source), go_down & (own_row < source))

    turns = steps + LAG * (planes - 1)

    def finish(turn, carry):
        right(turn, end, False)
        return carry

    for turn in range(AHEAD):
        right(jnp.int32(turn), start, True)
    for n in range(len(PAIRS)):
        off_line(n, start, True)
    for n, (row, col) in enumerate(PAIRS):
        block = corner[n]
        m[col * BS : (col + 1) * BS, row * BS : (row + 1) * BS] = block.T
        if row != col:
            m[row * BS : (row + 1) * BS, col * BS : (col + 1) * BS] = block
    factor(m, BS, PANELS, lambda index: right(index + AHEAD, start, True))
    for k in range(PANELS):
        rows = m[k * BS : (k + 1) * BS, :]
        lane = lax.broadcasted_iota(jnp.int32, rows.shape, 1)
        sub = lax.broadcasted_iota(jnp.int32, rows.shape, 0) + k * BS
        rows = jnp.where(lane > sub, 0.0, rows)
        top = rows.astype(jnp.bfloat16)
        high[k * BS : (k + 1) * BS, :] = top
        low[k * BS : (k + 1) * BS, :] = (rows - top.astype(jnp.float32)).astype(jnp.bfloat16)

    group = ratio * BS
    half = blocks * BS // 2
    first_update = turns - 2 * done

    def left_solve(i):
        for k in range(PANELS):
            step = i * PANELS + k

            @pl.when(jnp.logical_not(early(step)))
            def _():
                need_left(step)
        at = pl.ds(pl.multiple_of(i * BS, BS), BS)
        value = split(raw[0, at, :])
        for k in range(PANELS):
            size = (k + 1) * BS
            span = slice(k * BS, size)
            top, rest = split(product(
                (value[0][:, :size], value[1][:, :size]), (high[span, :size], low[span, :size]), NT
            ))
            left_high[at, span] = top
            left_low[at, span] = rest

    def right_solve(i, into_high, into_low):
        at = pl.ds(pl.multiple_of(i * BS, BS), BS)
        for t in range(ratio):
            root = own_row == own_col + grid_cols * t
            first = CORES * BS
            lanes_t = slice(t * BS, (t + 1) * BS)

            def keep(k, value):
                span = slice(k * BS, (k + 1) * BS)
                top, rest = split(value)
                into_high[span, lanes_t] = top
                into_low[span, lanes_t] = rest

            strips = (plane == 0) & jnp.logical_not(root)

            @pl.when(jnp.logical_not(strips))
            def _():
                vh, vl = split(raw[jnp.where(root, 0, 1 + t), at, :])
                for k in range(PANELS):
                    size = (k + 1) * BS
                    span = slice(k * BS, size)
                    keep(k, product((high[span, :size], low[span, :size]), (vh[:, :size], vl[:, :size]), NT))

            @pl.when(strips)
            def _():
                vh, vl = split(raw[1 + t, at, :])
                for k in range(PANELS):
                    size = (k + 1) * BS
                    span = slice(k * BS, size)
                    value = None
                    for b in range(min(k + 1, CORES)):
                        lane = slice(b * BS, (b + 1) * BS)
                        term = product((high[span, lane], low[span, lane]), (vh[:, lane], vl[:, lane]), NN)
                        value = term if value is None else value + term
                    if size > first:
                        lane = slice(first, size)
                        value = value + product(
                            (high[span, lane], low[span, lane]), (vh[:, lane], vl[:, lane]), NT
                        )
                    keep(k, value)

    def span_of(h):
        return (
            pl.ds(pl.multiple_of(lax.rem(h, 2) * half, half), half),
            pl.ds(pl.multiple_of(h // 2 * group, group), group),
        )

    def tile_in(h):
        slot = lax.rem(h, 2)
        return pltpu.make_async_copy(matrix.at[span_of(h)], tiles_in.at[slot], in_sem.at[slot])

    def tile_out(h):
        slot = lax.rem(h, 2)
        return pltpu.make_async_copy(tiles_out.at[slot], part.at[span_of(h)], out_sem.at[slot])

    def update_piece(h):
        slot = lax.rem(h, 2)

        @pl.when(h + 1 < 2 * done)
        def _():
            tile_in(h + 1).start()

        tile_in(h).wait()

        @pl.when(h >= 2)
        def _():
            tile_out(h - 2).wait()

        at = span_of(h)[0]
        tiles_out[slot] = tiles_in[slot] - product(
            (left_high[at, :], left_low[at, :]), (right_high[...], right_low[...]), NN
        )
        tile_out(h).start()

    def keep_left(high_not_low):
        src, dst = (left_high, left_high_out) if high_not_low else (left_low, left_low_out)
        return pltpu.make_async_copy(src, dst, left_out_sem.at[0 if high_not_low else 1])

    def keep_right(n, high_not_low):
        src, dst = (tail_high, right_high_out) if high_not_low else (tail_low, right_low_out)
        return pltpu.make_async_copy(src.at[n], dst.at[n], right_out_sem.at[n, 0 if high_not_low else 1])

    def go_on(turn, carry):
        right(turn, start, True)
        i = turn - first_left

        @pl.when((i >= 0) & (i < blocks))
        def _():
            left_solve(i)

        @pl.when(i == blocks - 1)
        def _():
            keep_left(True).start()
            keep_left(False).start()

        h = turn - first_update

        @pl.when(h == -1)
        def _():
            tile_in(0).start()

        @pl.when((h >= 0) & (lax.rem(h, 2) == 0))
        def _():
            right_solve(h // 2, right_high, right_low)

        @pl.when(h >= 0)
        def _():
            update_piece(h)

        for n in range(blocks - done):
            @pl.when(turn == (done + n + 1) * PANELS - 1 + LAG * (planes - 1))
            def _():
                right_solve(done + n, tail_high.at[n], tail_low.at[n])
                keep_right(n, True).start()
                keep_right(n, False).start()
        return carry

    assert first_left + blocks <= first_update + 1 and done * 2 >= 2
    lax.fori_loop(first_left - 1, turns, go_on, 0)
    for h in (2 * done - 2, 2 * done - 1):
        tile_out(jnp.int32(h)).wait()
    lax.fori_loop(0, turns, finish, 0)
    each_left(end, 0, blocks)
    each_strip(None, end)
    scatter(end)
    for n in range(len(PAIRS)):
        on_line(n, end, False)
        off_line(n, end, False)
    for high_not_low in (True, False):
        keep_left(high_not_low).wait()
        for n in range(blocks - done):
            keep_right(n, high_not_low).wait()


def exchange(grid_rows, grid_cols, done, matrix):
    rows = matrix.shape[0]
    blocks = rows // BS
    ratio = grid_rows // grid_cols
    steps = blocks * PANELS
    tiles = len(PAIRS)
    group = ratio * BS
    dma, half = pltpu.SemaphoreType.DMA, jnp.bfloat16
    in_hbm = pl.BlockSpec(memory_space=pltpu.HBM)
    left = jax.ShapeDtypeStruct((rows, WIDTH), half)
    right = jax.ShapeDtypeStruct((blocks - done, WIDTH, group), half)
    return pl.pallas_call(
        functools.partial(exchange_kernel, grid_rows, grid_cols, blocks, done),
        out_shape=(jax.ShapeDtypeStruct((rows, done * group), jnp.float32), left, left, right, right),
        in_specs=[in_hbm],
        out_specs=(in_hbm,) * 5,
        scratch_shapes=[
            pltpu.VMEM((1 + ratio, rows, WIDTH), jnp.float32),
            pltpu.VMEM((WIDTH, WIDTH), half),
            pltpu.VMEM((WIDTH, WIDTH), half),
            pltpu.VMEM((rows, WIDTH), half),
            pltpu.VMEM((rows, WIDTH), half),
            pltpu.VMEM((WIDTH, group), half),
            pltpu.VMEM((WIDTH, group), half),
            pltpu.VMEM((blocks - done, WIDTH, group), half),
            pltpu.VMEM((blocks - done, WIDTH, group), half),
            pltpu.VMEM((2, rows // 2, group), jnp.float32),
            pltpu.VMEM((2, rows // 2, group), jnp.float32),
            pltpu.VMEM((blocks, BS, BS), jnp.float32),
            pltpu.VMEM((tiles, BS, BS), jnp.float32),
            pltpu.VMEM((WIDTH, WIDTH), jnp.float32),
            dma,
            dma((grid_cols,)),
            dma((tiles, 1 + grid_cols)),
            dma((tiles, grid_cols)),
            dma((tiles, grid_cols)),
            dma((grid_cols, blocks)),
            dma((steps,)),
            dma((ratio, 3, steps)),
            dma((ratio, steps)),
            dma((blocks,)),
            dma((blocks,)),
            dma((ratio, blocks)),
            dma((ratio, blocks)),
            dma((2,)),
            dma((2,)),
            dma((2,)),
            dma((blocks - done, 2)),
        ],
        compiler_params=pltpu.CompilerParams(
            collective_id=0, has_side_effects=True, vmem_limit_bytes=60 << 20
        ),
        name="exchange",
    )(matrix)


def update_kernel(grid_rows, tail, place, part, *rest):
    matrices, (left_high, left_low, right_high, right_low, out) = rest[:tail], rest[tail:]
    own_row, own_col = place[0], place[1]
    i = pl.program_id(0)
    tile_rows, width = part.shape
    group = matrices[0].shape[1]
    lh, ll = left_high[...], left_low[...]
    out[:, :width] = part[...]
    for n in range(tail):
        at = slice(width + n * group, width + (n + 1) * group)
        out[:, at] = matrices[n][...] - product((lh, ll), (right_high[n], right_low[n]), NN)

    @pl.when((i == 0) & (own_row < PANELS))
    def _():
        out[:BS, :] = jnp.zeros((BS, out.shape[1]), jnp.float32)

    for k in range(PANELS):
        @pl.when(own_col == k)
        def _():
            span = slice(k * BS, (k + 1) * BS)
            row = lax.broadcasted_iota(jnp.int32, (tile_rows, BS), 0)
            lane = lax.broadcasted_iota(jnp.int32, (tile_rows, BS), 1)
            block = (i * (tile_rows // BS) + row // BS) * grid_rows + own_row
            kept = (block > k) | ((block == k) & (lane <= lax.rem(row, BS)))
            value = lh[:, span].astype(jnp.float32) + ll[:, span].astype(jnp.float32)
            out[:, :BS] = jnp.where(kept, value, 0.0)


def update(grid_rows, own_row, own_col, done, matrix, part, left_high, left_low, right_high, right_low):
    rows, cols = matrix.shape
    tail, _, group = right_high.shape
    tile_rows = min(2 * BS, rows)
    place = jnp.stack([own_row, own_col]).astype(jnp.int32)
    left_spec = pl.BlockSpec((tile_rows, WIDTH), lambda i, place: (i, 0))
    right_spec = pl.BlockSpec((tail, WIDTH, group), lambda i, place: (0, 0, 0))
    tail_specs = [pl.BlockSpec((tile_rows, group), lambda i, place, n=n: (i, done + n)) for n in range(tail)]
    return pl.pallas_call(
        functools.partial(update_kernel, grid_rows, tail),
        out_shape=jax.ShapeDtypeStruct(matrix.shape, jnp.float32),
        grid_spec=pltpu.PrefetchScalarGridSpec(
            num_scalar_prefetch=1,
            grid=(rows // tile_rows,),
            in_specs=[
                pl.BlockSpec((tile_rows, part.shape[1]), lambda i, place: (i, 0)),
                *tail_specs, left_spec, left_spec, right_spec, right_spec,
            ],
            out_specs=pl.BlockSpec((tile_rows, cols), lambda i, place: (i, 0)),
        ),
        compiler_params=pltpu.CompilerParams(
            dimension_semantics=("arbitrary",), vmem_limit_bytes=60 << 20
        ),
        name="update",
    )(place, part, *[matrix] * tail, left_high, left_low, right_high, right_low)


def on_device(gram):
    matrix = gram[0, 0]
    grid_rows = lax.axis_size("row")
    grid_cols = lax.axis_size("col")
    assert grid_rows % grid_cols == 0 and grid_cols % CORES == 0 and grid_cols >= PANELS
    blocks = matrix.shape[0] // BS
    done = blocks * 5 // 8
    parts = exchange(grid_rows, grid_cols, done, matrix)
    result = update(grid_rows, lax.axis_index("row"), lax.axis_index("col"), done, matrix, *parts)
    return result[None, None]


def solution(mesh):
    in_specs = (P("row", "col", None, None),)
    out_specs = P("row", "col", None, None)
    return jax.shard_map(
        on_device, mesh=mesh, in_specs=in_specs, out_specs=out_specs, check_vma=False
    )
```

```python
import functools

import jax
import jax.numpy as jnp
from jax import lax
from jax.experimental import pallas as pl
from jax.experimental.pallas import tpu as pltpu
from jax.sharding import PartitionSpec as P

BS = 256
PANELS = 3
WIDTH = BS * PANELS
GROUP = 64
CORES = 2
LAG = 2
AHEAD = 3
HI = lax.Precision.HIGHEST
MESH = pl.DeviceIdType.MESH
PAIRS = [(row, col) for col in range(PANELS) for row in range(col, PANELS)]


def lanes(col):
    return jnp.broadcast_to(col, (8, 128))

def eliminate(x, width):
    lane = lax.broadcasted_iota(jnp.int32, (8, 128), 1)
    sub = lax.broadcasted_iota(jnp.int32, (8, 128), 0)
    n = GROUP // 8
    nl = width // 128
    v = [[x[8*r:8*r+8, 128*l:128*l+128] for l in range(nl)] for r in range(n)]
    for r in range(n):
        base = 8 * r
        cols = {q: [lanes(v[q][0][:, base+j:base+j+1]) for j in range(8)] for q in range(r, n)}
        s = {(i, l): lanes(cols[r][l][i:i+1, :]) for i in range(8) for l in range(i, 8)}
        rows = [[lanes(v[r][l][j:j+1, :]) for l in range(nl)] for j in range(8)]
        inv = []
        unit = {}
        mult = {}
        for j in range(8):
            d = s[j, j]
            inv.append(recip(d))
            for i in range(j + 1, 8):
                f = s[j, i] * inv[j]
                mult[i, j] = f
                for l in range(i, 8):
                    s[i, l] = s[i, l] - f * s[j, l]
        for i in range(8):
            for l in range(i):
                t = mult[i, l]
                for m in range(l + 1, i):
                    t = t + mult[i, m] * unit[m, l]
                unit[i, l] = -t
        wcol = []
        for j in range(8):
            t = jnp.where(sub == j, 1.0, 0.0)
            for i in range(j + 1, 8):
                t = jnp.where(sub == i, unit[i, j], t)
            wcol.append(t)
        dvec = s[0, 0]
        for j in range(1, 8):
            dvec = jnp.where(sub == j, s[j, j], dvec)
        scale = lax.rsqrt(dvec)
        ident = [jnp.where((lane >= base) & (lane < base + 8), jnp.where(lane == base + j, 1.0, 0.0), rows[j][0]) for j in range(8)]
        for q in range(r + 1, n):
            c = list(cols[q])
            f = []
            for j in range(8):
                fj = c[j] * inv[j]
                f.append(fj)
                for l in range(j + 1, 8):
                    c[l] = c[l] - fj * s[j, l]
            first = jnp.where((lane >= base) & (lane < base + 8), 0.0, v[q][0])
            acc = [first] + [v[q][l] for l in range(1, nl)]
            for j in range(8):
                g = f[j]
                for i in range(j + 1, 8):
                    g = g + f[i] * unit[i, j]
                acc[0] = acc[0] - g * ident[j]
                for l in range(1, nl):
                    acc[l] = acc[l] - g * rows[j][l]
            v[q] = acc
        new = []
        for l in range(nl):
            t = wcol[0] * (ident[0] if l == 0 else rows[0][l])
            for j in range(1, 8):
                t = t + wcol[j] * (ident[j] if l == 0 else rows[j][l])
            new.append(t * scale)
        upper = wcol[0] * rows[0][0]
        for j in range(1, 8):
            upper = upper + wcol[j] * rows[j][0]
        keep = (lane > base + sub) & (lane < base + 8)
        new[0] = jnp.where(keep, upper * scale, new[0])
        v[r] = new
    return jnp.concatenate([jnp.concatenate(t, axis=1) for t in v], axis=0)

def recip(d):
    r = pl.reciprocal(d, approx=True)
    r = r * (2.0 - d * r)
    return r

def factor(m, bs, panels, hook=None):
    width = bs * panels
    groups = bs // GROUP
    for k in range(panels):
        def body(g, carry):
            start = pl.multiple_of(k * bs + g * GROUP, GROUP)
            rows = m[pl.ds(start, GROUP), :]
            x = pltpu.roll(rows, width - start, axis=1)
            x = eliminate(x, width)
            x = pltpu.roll(x, start, axis=1)
            m[pl.ds(start, GROUP), :] = x
            lane = lax.broadcasted_iota(jnp.int32, (GROUP, width), 1)
            sub = lax.broadcasted_iota(jnp.int32, (GROUP, width), 0)
            upd = jnp.where((lane - start > sub) & (lane < start + GROUP), 0.0, x)
            own = x[:, k*bs:(k+1)*bs]
            lane_own = lax.broadcasted_iota(jnp.int32, (GROUP, bs), 1) + k * bs
            left = jnp.where(lane_own >= start + GROUP, own, 0.0)
            prod = lax.dot_general(left, upd, (((0,), (0,)), ((), ())), precision=HI, preferred_element_type=jnp.float32)
            old = m[k*bs:(k+1)*bs, :]
            r2 = lax.broadcasted_iota(jnp.int32, (bs, width), 0) + k * bs
            l2 = lax.broadcasted_iota(jnp.int32, (bs, width), 1)
            old = jnp.where((r2 >= start + GROUP) & (l2 >= start) & (l2 < start + GROUP), 0.0, old)
            m[k*bs:(k+1)*bs, :] = old - prod
            if hook is not None: hook(k * groups + g)
            return carry
        lax.fori_loop(0, groups, body, 0)
        if k + 1 < panels:
            full = m[k*bs:(k+1)*bs, :]
            l2 = lax.broadcasted_iota(jnp.int32, (bs, width), 1)
            r2 = lax.broadcasted_iota(jnp.int32, (bs, width), 0) + k * bs
            upd = jnp.where((l2 > r2) & (l2 < (k+1)*bs), 0.0, full)
            for r in range(k + 1, panels):
                left = m[k*bs:(k+1)*bs, r*bs:(r+1)*bs]
                prod = lax.dot_general(left, upd, (((0,), (0,)), ((), ())), precision=HI, preferred_element_type=jnp.float32)
                if k > 0:
                    m[r*bs:(r+1)*bs, :k*bs] -= prod[:, :k*bs]
                m[r*bs:(r+1)*bs, k*bs:(k+1)*bs] = -prod[:, k*bs:(k+1)*bs]
                m[r*bs:(r+1)*bs, (k+1)*bs:] -= prod[:, (k+1)*bs:]

def split(value):
    high = value.astype(jnp.bfloat16)
    return high, (value - high.astype(jnp.float32)).astype(jnp.bfloat16)


def wide(left, right, dims):
    return lax.dot_general(left, right, (dims, ((), ())), preferred_element_type=jnp.float32)


NT = ((1,), (1,))
NN = ((1,), (0,))


def product(left, right, dims):
    (lh, ll), (rh, rl) = left, right
    return wide(lh, rh, dims) + wide(lh, rl, dims) + wide(ll, rh, dims)


def exchange_kernel(
    grid_rows, grid_cols, blocks, done, matrix, part, left_high_out, left_low_out, right_high_out, right_low_out,
    raw, high, low, left_high, left_low, right_high, right_low, tail_high, tail_low, tiles_in, tiles_out,
    spare, corner, m, stage_sem, scatter_send, fan_send, core_send, corner_recv,
    left_send, left_recv, right_send, right_recv, spare_send, spare_recv, strip_keep, strip_send, in_sem, out_sem, left_out_sem, right_out_sem,
):
    own_row, own_col = lax.axis_index("row"), lax.axis_index("col")
    ratio = grid_rows // grid_cols
    core = lax.rem(own_row, CORES)
    plane, planes = own_row // CORES, grid_rows // CORES
    steps = blocks * PANELS
    has_up, has_down = plane + 1 < planes, plane > 0
    up = jnp.minimum(own_row + CORES, grid_rows - CORES + core)
    down = jnp.maximum(own_row - CORES, core)
    partner = own_row + 1 - 2 * core

    def beside(other):
        return lax.rem(own_col + other, grid_cols)

    barrier = pltpu.get_barrier_semaphore()
    for other in range(1, grid_cols):
        pl.semaphore_signal(barrier, inc=1, device_id=(own_row, beside(other)), device_id_type=MESH)
    pl.semaphore_signal(barrier, inc=1, device_id=(partner, own_col), device_id_type=MESH)

    @pl.when(has_up)
    def _():
        pl.semaphore_signal(barrier, inc=1, device_id=(up, own_col), device_id_type=MESH)

    @pl.when(has_down)
    def _():
        pl.semaphore_signal(barrier, inc=1, device_id=(down, own_col), device_id_type=MESH)

    pl.semaphore_wait(barrier, grid_cols + has_up.astype(jnp.int32) + has_down.astype(jnp.int32))

    def copy(src, dst, send, recv, row, col):
        return pltpu.make_async_remote_copy(
            src_ref=src, dst_ref=dst, send_sem=send, recv_sem=recv,
            device_id=(row, col), device_id_type=MESH,
        )

    for k in range(PANELS):
        @pl.when(own_col == k)
        def _():
            pltpu.make_async_copy(matrix.at[:, 0:BS], raw.at[0, :, k * BS : (k + 1) * BS], stage_sem).start()

    size = BS // grid_cols

    def part_of(n, j):
        span = pl.ds(pl.multiple_of(j * size, 8), size)
        return span, corner.at[n, span], corner_recv.at[n, j]

    def scatter(act):
        for n, (row, col) in enumerate(PAIRS):
            @pl.when((own_row == row) & (own_col == col))
            def _():
                for other in range(1, grid_cols):
                    j = beside(other)
                    span, here, recv = part_of(n, j)
                    act(copy(matrix.at[span, 0:BS], here, scatter_send.at[other], recv, own_row, j))

    def on_line(n, act, wait):
        row, col = PAIRS[n]

        @pl.when(core == row % CORES)
        def _():
            span, here, recv = part_of(n, own_col)
            source = (own_row == row) & (own_col == col)

            def fan(src):
                @pl.when(has_up & (own_row >= row))
                def _():
                    act(copy(src, here, fan_send.at[n, 0], recv, up, own_col))

                @pl.when(has_down & (own_row <= row))
                def _():
                    act(copy(src, here, fan_send.at[n, grid_cols], recv, down, own_col))

                for other in range(1, grid_cols):
                    act(copy(src, here, fan_send.at[n, other], recv, own_row, beside(other)))
                act(copy(src, here, core_send.at[n, own_col], recv, partner, own_col))

            @pl.when(source)
            def _():
                fan(matrix.at[span, 0:BS])

            @pl.when(jnp.logical_not(source))
            def _():
                if wait:
                    copy(here, here, core_send.at[n, own_col], recv, partner, own_col).wait_recv()
                fan(here)

    def off_line(n, act, wait):
        primary = core == PAIRS[n][0] % CORES

        def one(j, carry):
            span, here, recv = part_of(n, j)
            c = copy(here, here, core_send.at[n, j], recv, partner, own_col)

            @pl.when((j != own_col) | jnp.logical_not(primary))
            def _():
                if wait:
                    c.wait_recv()

                @pl.when(primary)
                def _():
                    act(c)
            return carry

        lax.fori_loop(0, grid_cols, one, 0)

    def start(c):
        c.start()

    def end(c):
        c.wait_send()

    root_col = lax.rem(own_row, grid_cols)
    spare_col = lax.rem(root_col + grid_cols // 2, grid_cols)

    def tile(slot, i, k):
        return raw.at[slot, pl.ds(pl.multiple_of(i * BS, BS), BS), pl.ds(pl.multiple_of(k * BS, BS), BS)]

    def each_left(act, first, last):
        def one(i, carry):
            for other in range(grid_cols):
                col = lax.rem(root_col + other, grid_cols)
                for k in range(PANELS):
                    @pl.when((own_col == k) & (col != own_col))
                    def _():
                        here = tile(0, i, k)
                        act(copy(here, here, left_send.at[other, i], left_recv.at[i * PANELS + k], own_row, col))
            return carry
        lax.fori_loop(first, last, one, 0)

    scatter(start)

    @pl.when(own_col < PANELS)
    def _():
        pltpu.make_async_copy(matrix.at[:, 0:BS], raw.at[0, :, 0:BS], stage_sem).wait()

    each_left(start, 0, 1)
    for n in range(len(PAIRS)):
        on_line(n, start, True)
    each_left(start, 1, blocks)

    def each_strip(keep, act):
        def one(i, carry):
            for k in range(CORES):
                @pl.when(own_row == k)
                def _():
                    for t in range(ratio):
                        c = pl.multiple_of((t + i * ratio) * BS, BS)
                        src, here = matrix.at[0:BS, pl.ds(c, BS)], tile(1 + t, i, k)

                        @pl.when(own_row != own_col + grid_cols * t)
                        def _():
                            if keep is not None:
                                keep(pltpu.make_async_copy(src, here, strip_keep.at[t, i]))

                        @pl.when(partner != own_col + grid_cols * t)
                        def _():
                            act(copy(
                                src, here, strip_send.at[t, i], right_recv.at[t, i * PANELS + k], partner, own_col
                            ))
            return carry
        lax.fori_loop(0, blocks, one, 0)

    each_strip(start, start)

    for n, (row, col) in enumerate(PAIRS):
        @pl.when((own_row == row) & (own_col == col))
        def _():
            span, here, recv = part_of(n, own_col)
            keep = pltpu.make_async_copy(matrix.at[span, 0:BS], here, stage_sem)
            keep.start()
            keep.wait()


    active = core == lax.rem(own_col, CORES)
    divert = ratio > 1 and planes > CORES
    spare_step = jnp.minimum(spare_col, PANELS - 1)
    is_source = (own_col == spare_col) & (plane == planes - 2)
    is_spare = (own_col == lax.rem(down + grid_cols // 2, grid_cols)) & (plane == planes - 1)
    home = lax.rem(down, grid_cols)

    is_root = own_col == root_col
    first_left = AHEAD + PANELS * (BS // GROUP) + 1

    def early(step):
        passed_on = is_root
        if divert:
            passed_on = passed_on | (is_source & (lax.rem(step, PANELS) == spare_step))
        return passed_on & (step <= first_left + step // PANELS // 2)

    def need_left(step):
        k = lax.rem(step, PANELS)

        @pl.when(own_col != k)
        def _():
            here = tile(0, step // PANELS, k)
            copy(here, here, left_send.at[0, 0], left_recv.at[step], partner, own_col).wait_recv()

    def right(turn, act, wait):
        if wait:
            @pl.when((turn < steps) & early(turn))
            def _():
                need_left(turn)
        if divert:
            i, k = turn // PANELS, lax.rem(turn, PANELS)

            @pl.when(is_source & (turn < steps) & (k == spare_step))
            def _():
                act(copy(tile(0, i, k), spare.at[i], spare_send.at[i], spare_recv.at[i], up, own_col))

            late = turn - LAG
            i, k = late // PANELS, lax.rem(late, PANELS)

            @pl.when(is_spare & (late >= 0) & (late < steps) & (k == jnp.minimum(own_col, PANELS - 1)))
            def _():
                here = spare.at[i]
                if wait:
                    copy(here, here, spare_send.at[i], spare_recv.at[i], partner, own_col).wait_recv()
                slot = down // grid_cols
                for t in range(ratio):
                    @pl.when(slot == t)
                    def _():
                        act(copy(here, tile(1 + t, i, k), spare_send.at[i], right_recv.at[t, late], own_row, home))
        for t in range(ratio):
            source = own_col + grid_cols * t
            root = own_row == source
            level = source // CORES
            step = turn - LAG * jnp.abs(plane - level)

            @pl.when((step >= 0) & (step < steps))
            def _():
                i, k = step // PANELS, lax.rem(step, PANELS)
                here = tile(1 + t, i, k)

                def send(src, index, to_row):
                    act(copy(
                        src, here, right_send.at[t, index, step], right_recv.at[t, step], to_row, own_col
                    ))

                def fan(src, go_up, go_down):
                    @pl.when(go_up)
                    def _():
                        send(src, 0, up)

                    @pl.when(go_down)
                    def _():
                        send(src, 1, down)

                    @pl.when((plane > 0) | (k >= CORES))
                    def _():
                        send(src, 2, partner)

                strips = (plane == 0) & (k < CORES)
                go_down = (plane > 1) | ((plane == 1) & (k >= CORES))

                @pl.when(root)
                def _():
                    go_up = has_up
                    if divert:
                        go_up = has_up & jnp.logical_not((k == spare_step) & (plane == planes - 2))
                    fan(tile(0, i, k), go_up, go_down)

                @pl.when(jnp.logical_not(root))
                def _():
                    if wait:
                        local = strips & (k == own_row)

                        @pl.when(local)
                        def _():
                            pltpu.make_async_copy(here, here, strip_keep.at[t, i]).wait()

                        @pl.when(jnp.logical_not(local))
                        def _():
                            copy(
                                here, here, right_send.at[t, 2, step], right_recv.at[t, step], partner, own_col
                            ).wait_recv()

                    @pl.when(active)
                    def _():
                        fan(here, has_up & (own_row > source), go_down & (own_row < source))

    turns = steps + LAG * (planes - 1)

    def finish(turn, carry):
        right(turn, end, False)
        return carry

    for turn in range(AHEAD):
        right(jnp.int32(turn), start, True)
    for n in range(len(PAIRS)):
        off_line(n, start, True)
    for n, (row, col) in enumerate(PAIRS):
        block = corner[n]
        m[col * BS : (col + 1) * BS, row * BS : (row + 1) * BS] = block.T
        if row != col:
            m[row * BS : (row + 1) * BS, col * BS : (col + 1) * BS] = block
    factor(m, BS, PANELS, lambda index: right(index + AHEAD, start, True))
    for k in range(PANELS):
        rows = m[k * BS : (k + 1) * BS, :]
        lane = lax.broadcasted_iota(jnp.int32, rows.shape, 1)
        sub = lax.broadcasted_iota(jnp.int32, rows.shape, 0) + k * BS
        rows = jnp.where(lane > sub, 0.0, rows)
        top = rows.astype(jnp.bfloat16)
        high[k * BS : (k + 1) * BS, :] = top
        low[k * BS : (k + 1) * BS, :] = (rows - top.astype(jnp.float32)).astype(jnp.bfloat16)

    group = ratio * BS
    half = blocks * BS // 2
    first_update = max(turns - 2 * done, first_left + blocks // 2)

    def left_solve(i):
        for k in range(PANELS):
            step = i * PANELS + k

            @pl.when(jnp.logical_not(early(step)))
            def _():
                need_left(step)
        at = pl.ds(pl.multiple_of(i * BS, BS), BS)
        value = split(raw[0, at, :])
        for k in range(PANELS):
            size = (k + 1) * BS
            span = slice(k * BS, size)
            top, rest = split(product(
                (value[0][:, :size], value[1][:, :size]), (high[span, :size], low[span, :size]), NT
            ))
            left_high[at, span] = top
            left_low[at, span] = rest

    def right_solve(i, into_high, into_low):
        at = pl.ds(pl.multiple_of(i * BS, BS), BS)
        for t in range(ratio):
            root = own_row == own_col + grid_cols * t
            first = CORES * BS
            lanes_t = slice(t * BS, (t + 1) * BS)

            def keep(k, value):
                span = slice(k * BS, (k + 1) * BS)
                top, rest = split(value)
                into_high[span, lanes_t] = top
                into_low[span, lanes_t] = rest

            strips = (plane == 0) & jnp.logical_not(root)

            @pl.when(jnp.logical_not(strips))
            def _():
                vh, vl = split(raw[jnp.where(root, 0, 1 + t), at, :])
                for k in range(PANELS):
                    size = (k + 1) * BS
                    span = slice(k * BS, size)
                    keep(k, product((high[span, :size], low[span, :size]), (vh[:, :size], vl[:, :size]), NT))

            @pl.when(strips)
            def _():
                vh, vl = split(raw[1 + t, at, :])
                for k in range(PANELS):
                    size = (k + 1) * BS
                    span = slice(k * BS, size)
                    value = None
                    for b in range(min(k + 1, CORES)):
                        lane = slice(b * BS, (b + 1) * BS)
                        term = product((high[span, lane], low[span, lane]), (vh[:, lane], vl[:, lane]), NN)
                        value = term if value is None else value + term
                    if size > first:
                        lane = slice(first, size)
                        value = value + product(
                            (high[span, lane], low[span, lane]), (vh[:, lane], vl[:, lane]), NT
                        )
                    keep(k, value)

    def span_of(h):
        return (
            pl.ds(pl.multiple_of(lax.rem(h, 2) * half, half), half),
            pl.ds(pl.multiple_of(h // 2 * group, group), group),
        )

    def tile_in(h):
        slot = lax.rem(h, 2)
        return pltpu.make_async_copy(matrix.at[span_of(h)], tiles_in.at[slot], in_sem.at[slot])

    def tile_out(h):
        slot = lax.rem(h, 2)
        return pltpu.make_async_copy(tiles_out.at[slot], part.at[span_of(h)], out_sem.at[slot])

    def update_piece(h):
        slot = lax.rem(h, 2)

        @pl.when(h + 1 < 2 * done)
        def _():
            tile_in(h + 1).start()

        tile_in(h).wait()

        @pl.when(h >= 2)
        def _():
            tile_out(h - 2).wait()

        at = span_of(h)[0]
        tiles_out[slot] = tiles_in[slot] - product(
            (left_high[at, :], left_low[at, :]), (right_high[...], right_low[...]), NN
        )
        tile_out(h).start()

    def keep_left(high_not_low):
        src, dst = (left_high, left_high_out) if high_not_low else (left_low, left_low_out)
        return pltpu.make_async_copy(src, dst, left_out_sem.at[0 if high_not_low else 1])

    def keep_right(n, high_not_low):
        src, dst = (tail_high, right_high_out) if high_not_low else (tail_low, right_low_out)
        return pltpu.make_async_copy(src.at[n], dst.at[n], right_out_sem.at[n, 0 if high_not_low else 1])

    def go_on(turn, carry):
        right(turn, start, True)
        i = 2 * (turn - first_left)

        def pair(n, carry):
            left_solve(i + n)
            return carry

        @pl.when((i >= 0) & (i < blocks))
        def _():
            lax.fori_loop(0, 2, pair, 0)

        @pl.when(i == blocks - 2)
        def _():
            keep_left(True).start()
            keep_left(False).start()

        h = turn - first_update

        @pl.when(h == -1)
        def _():
            tile_in(0).start()

        @pl.when((h >= 0) & (h < 2 * done) & (lax.rem(h, 2) == 0))
        def _():
            right_solve(h // 2, right_high, right_low)

        @pl.when((h >= 0) & (h < 2 * done))
        def _():
            update_piece(h)

        for n in range(blocks - done):
            @pl.when(turn == (done + n + 1) * PANELS - 1 + LAG * (planes - 1))
            def _():
                right_solve(done + n, tail_high.at[n], tail_low.at[n])
                keep_right(n, True).start()
                keep_right(n, False).start()
        return carry

    assert blocks % 2 == 0 and done >= 1
    lax.fori_loop(first_left - 1, max(turns, first_update + 2 * done), go_on, 0)
    for h in (2 * done - 2, 2 * done - 1):
        tile_out(jnp.int32(h)).wait()
    lax.fori_loop(0, turns, finish, 0)
    each_left(end, 0, blocks)
    each_strip(None, end)
    scatter(end)
    for n in range(len(PAIRS)):
        on_line(n, end, False)
        off_line(n, end, False)
    for high_not_low in (True, False):
        keep_left(high_not_low).wait()
        for n in range(blocks - done):
            keep_right(n, high_not_low).wait()


def exchange(grid_rows, grid_cols, done, matrix):
    rows = matrix.shape[0]
    blocks = rows // BS
    ratio = grid_rows // grid_cols
    steps = blocks * PANELS
    tiles = len(PAIRS)
    group = ratio * BS
    dma, half = pltpu.SemaphoreType.DMA, jnp.bfloat16
    in_hbm = pl.BlockSpec(memory_space=pltpu.HBM)
    left = jax.ShapeDtypeStruct((rows, WIDTH), half)
    right = jax.ShapeDtypeStruct((blocks - done, WIDTH, group), half)
    return pl.pallas_call(
        functools.partial(exchange_kernel, grid_rows, grid_cols, blocks, done),
        out_shape=(jax.ShapeDtypeStruct((rows, done * group), jnp.float32), left, left, right, right),
        in_specs=[in_hbm],
        out_specs=(in_hbm,) * 5,
        scratch_shapes=[
            pltpu.VMEM((1 + ratio, rows, WIDTH), jnp.float32),
            pltpu.VMEM((WIDTH, WIDTH), half),
            pltpu.VMEM((WIDTH, WIDTH), half),
            pltpu.VMEM((rows, WIDTH), half),
            pltpu.VMEM((rows, WIDTH), half),
            pltpu.VMEM((WIDTH, group), half),
            pltpu.VMEM((WIDTH, group), half),
            pltpu.VMEM((blocks - done, WIDTH, group), half),
            pltpu.VMEM((blocks - done, WIDTH, group), half),
            pltpu.VMEM((2, rows // 2, group), jnp.float32),
            pltpu.VMEM((2, rows // 2, group), jnp.float32),
            pltpu.VMEM((blocks, BS, BS), jnp.float32),
            pltpu.VMEM((tiles, BS, BS), jnp.float32),
            pltpu.VMEM((WIDTH, WIDTH), jnp.float32),
            dma,
            dma((grid_cols,)),
            dma((tiles, 1 + grid_cols)),
            dma((tiles, grid_cols)),
            dma((tiles, grid_cols)),
            dma((grid_cols, blocks)),
            dma((steps,)),
            dma((ratio, 3, steps)),
            dma((ratio, steps)),
            dma((blocks,)),
            dma((blocks,)),
            dma((ratio, blocks)),
            dma((ratio, blocks)),
            dma((2,)),
            dma((2,)),
            dma((2,)),
            dma((blocks - done, 2)),
        ],
        compiler_params=pltpu.CompilerParams(
            collective_id=0, has_side_effects=True, vmem_limit_bytes=60 << 20
        ),
        name="exchange",
    )(matrix)


def update_kernel(grid_rows, tail, place, part, *rest):
    matrices, (left_high, left_low, right_high, right_low, out) = rest[:tail], rest[tail:]
    own_row, own_col = place[0], place[1]
    i = pl.program_id(0)
    tile_rows, width = part.shape
    group = matrices[0].shape[1]
    lh, ll = left_high[...], left_low[...]
    out[:, :width] = part[...]
    for n in range(tail):
        at = slice(width + n * group, width + (n + 1) * group)
        out[:, at] = matrices[n][...] - product((lh, ll), (right_high[n], right_low[n]), NN)

    @pl.when((i == 0) & (own_row < PANELS))
    def _():
        out[:BS, :] = jnp.zeros((BS, out.shape[1]), jnp.float32)

    for k in range(PANELS):
        @pl.when(own_col == k)
        def _():
            span = slice(k * BS, (k + 1) * BS)
            row = lax.broadcasted_iota(jnp.int32, (tile_rows, BS), 0)
            lane = lax.broadcasted_iota(jnp.int32, (tile_rows, BS), 1)
            block = (i * (tile_rows // BS) + row // BS) * grid_rows + own_row
            kept = (block > k) | ((block == k) & (lane <= lax.rem(row, BS)))
            value = lh[:, span].astype(jnp.float32) + ll[:, span].astype(jnp.float32)
            out[:, :BS] = jnp.where(kept, value, 0.0)


def update(grid_rows, own_row, own_col, done, matrix, part, left_high, left_low, right_high, right_low):
    rows, cols = matrix.shape
    tail, _, group = right_high.shape
    tile_rows = min(2 * BS, rows)
    place = jnp.stack([own_row, own_col]).astype(jnp.int32)
    left_spec = pl.BlockSpec((tile_rows, WIDTH), lambda i, place: (i, 0))
    right_spec = pl.BlockSpec((tail, WIDTH, group), lambda i, place: (0, 0, 0))
    tail_specs = [pl.BlockSpec((tile_rows, group), lambda i, place, n=n: (i, done + n)) for n in range(tail)]
    return pl.pallas_call(
        functools.partial(update_kernel, grid_rows, tail),
        out_shape=jax.ShapeDtypeStruct(matrix.shape, jnp.float32),
        grid_spec=pltpu.PrefetchScalarGridSpec(
            num_scalar_prefetch=1,
            grid=(rows // tile_rows,),
            in_specs=[
                pl.BlockSpec((tile_rows, part.shape[1]), lambda i, place: (i, 0)),
                *tail_specs, left_spec, left_spec, right_spec, right_spec,
            ],
            out_specs=pl.BlockSpec((tile_rows, cols), lambda i, place: (i, 0)),
        ),
        compiler_params=pltpu.CompilerParams(
            dimension_semantics=("arbitrary",), vmem_limit_bytes=60 << 20
        ),
        name="update",
    )(place, part, *[matrix] * tail, left_high, left_low, right_high, right_low)


def on_device(gram):
    matrix = gram[0, 0]
    grid_rows = lax.axis_size("row")
    grid_cols = lax.axis_size("col")
    assert grid_rows % grid_cols == 0 and grid_cols % CORES == 0 and grid_cols >= PANELS
    blocks = matrix.shape[0] // BS
    done = blocks * 5 // 8
    parts = exchange(grid_rows, grid_cols, done, matrix)
    result = update(grid_rows, lax.axis_index("row"), lax.axis_index("col"), done, matrix, *parts)
    return result[None, None]


def solution(mesh):
    in_specs = (P("row", "col", None, None),)
    out_specs = P("row", "col", None, None)
    return jax.shard_map(
        on_device, mesh=mesh, in_specs=in_specs, out_specs=out_specs, check_vma=False
    )
```
